32 devices in a mesh: tile: 2 (over y), date: 4 (over z), rng: 2 (over x), az: 2 (over core).
Axes of the slice: x: 2, y: 2, z: 4, core: 2. Of those that a mesh axis runs over, the one named last changes fastest.
Arguments:
- acquisitions: bfloat16 [32, 256, 2, 512], P(('tile', 'date'), 'az', None, 'rng'), parts along dimension 0, may hold values from -80 to 80
- date_pairs: int32 [2, 32], P(None, ('date', 'rng', 'az')), may hold values from 0 to 15, as said below
Outputs:
- filtered: bfloat16 [64, 2, 64, 32], P(('tile', 'date', 'rng', 'az')), parts along dimension 0
- coherence: bfloat16 [64, 64, 32], P(('tile', 'date', 'rng', 'az')), parts along dimension 0
The draws below stay inside these ranges and needn't reach their ends.
There are 2 independent parts, one for each index of `tile`. The reference program is written for one: setup_inputs(seed, part) draws one part's arguments, and reference() takes and returns one part's arrays. A program takes and returns all parts, laid end to end along the dimension named above; an argument that names none is the same for every part. Nothing has to cross between parts.
Inputs may be any that keep to these rules, and one draw needn't show every extreme that they name: For every column p, date_pairs[0,p] < date_pairs[1,p] <= date_pairs[0,p] + 8; some dates appear in many more pairs than others.
All inputs are finite; a program needn't handle non-finite values.
Results may differ from the reference program's by a relative error of at most 0.001.
Values may be sent and summed in bfloat16 or wider, within the bound.
No kernel may reach another device: no remote copies, remote signals or barrier semaphores. Data moves between devices by JAX's collectives and lax.ppermute only.
A program may use at most 64 MiB of HBM per device.

```python
import math
import jax
import jax.numpy as jnp
from jax import lax

PATCH = 64
LOOK_AZ = 4
LOOK_RG = 16
SPAN = 8
DATES = 16
PAIRS = 32
AZ = 256
RG = 512
HALF = 32
ML_AZ = 64
ML_RG = 32


def draw_acquisitions(key, part):
    key_common, key_speckle, key_screen = jax.random.split(jax.random.fold_in(key, 11), 3)
    look_lines = AZ // LOOK_AZ
    look_samples = RG // LOOK_RG
    common = jax.random.truncated_normal(key_common, -4.0, 4.0, (look_lines, LOOK_AZ, 2, look_samples, LOOK_RG), jnp.float32)
    speckle = jax.random.truncated_normal(key_speckle, -4.0, 4.0, (DATES, look_lines, LOOK_AZ, 2, look_samples, LOOK_RG), jnp.float32)
    phase_screen = jax.random.uniform(key_screen, (DATES, look_lines, 1, look_samples, 1), jnp.float32, -math.pi, math.pi)
    cosine_value = jnp.cos(phase_screen)
    sine_value = jnp.sin(phase_screen)
    common_real = common[:, :, 0][None]
    common_imag = common[:, :, 1][None]
    rotated_real = common_real * cosine_value - common_imag * sine_value
    rotated_imag = common_real * sine_value + common_imag * cosine_value
    strength = 0.8
    signal = jnp.stack([rotated_real, rotated_imag], axis=3) * strength + 0.6 * speckle
    return signal.reshape(DATES, AZ, 2, RG).astype(jnp.bfloat16)


def draw_date_pairs(key, part):
    key_one, key_two, key_spacing = jax.random.split(jax.random.fold_in(key, 23), 3)
    earlier = jnp.minimum(jax.random.randint(key_one, (PAIRS,), 0, DATES - SPAN, jnp.int32), jax.random.randint(key_two, (PAIRS,), 0, DATES - SPAN, jnp.int32))
    spacing = jax.random.randint(key_spacing, (PAIRS,), 1, SPAN + 1, jnp.int32)
    earlier = earlier.at[0].set(DATES - 1 - SPAN).at[PAIRS - 1].set(0)
    spacing = spacing.at[0].set(SPAN)
    return jnp.stack([earlier, earlier + spacing]).astype(jnp.int32)


def setup_inputs(seed: int = 0, part: int = 0) -> dict:
    key_list = jax.random.split(jax.random.key(seed), 3)
    part_splits = jax.random.split(jax.random.fold_in(key_list[2], part), 3)
    acquisitions = draw_acquisitions(jax.random.fold_in(jax.random.fold_in(key_list[2], part), 71), part)
    date_pairs = draw_date_pairs(jax.random.fold_in(key_list[2], 71), part)
    return {"acquisitions": acquisitions, "date_pairs": date_pairs}


EPSILON = 1e-06

def take_looks(values):
    shaped = values.reshape(ML_AZ, LOOK_AZ, ML_RG, LOOK_RG)
    return lax.optimization_barrier(jnp.sum(shaped, axis=(1, 3))) * (1.0 / (LOOK_AZ * LOOK_RG))

def date_power(acquisition):
    widened = acquisition.astype(jnp.float32)
    return take_looks(widened[:, 0, :] * widened[:, 0, :] + widened[:, 1, :] * widened[:, 1, :])

def taper_window():
    position = jnp.arange(PATCH, dtype=jnp.float32)
    ramp_line = 1.0 - jnp.abs(position + 0.5 - HALF) / HALF
    return ramp_line[:, None] * ramp_line[None, :]

def goldstein(ratio_real, ratio_imag):
    padded = lax.complex(jnp.pad(ratio_real, HALF), jnp.pad(ratio_imag, HALF))
    extent_line = padded.shape[0]
    extent_sample = padded.shape[1]
    summed = jnp.zeros_like(padded)
    window = taper_window()
    for start_line in (0, HALF):
        for start_sample in (0, HALF):
            count_line = (extent_line - start_line) // PATCH
            count_sample = (extent_sample - start_sample) // PATCH
            region = padded[start_line:start_line + count_line * PATCH, start_sample:start_sample + count_sample * PATCH]
            patches = region.reshape(count_line, PATCH, count_sample, PATCH).transpose(0, 2, 1, 3)
            spectrum = jnp.fft.fft2(patches)
            energy = spectrum.real * spectrum.real + spectrum.imag * spectrum.imag
            weight = (energy + 1.0) ** 0.25
            weight = weight / lax.optimization_barrier(jnp.mean(weight, axis=(2, 3), keepdims=True))
            shaped = jnp.fft.ifft2(spectrum * weight) * window
            placed = shaped.transpose(0, 2, 1, 3).reshape(count_line * PATCH, count_sample * PATCH)
            summed = summed.at[start_line:start_line + count_line * PATCH, start_sample:start_sample + count_sample * PATCH].add(placed)
    center = summed[HALF:HALF + ML_AZ, HALF:HALF + ML_RG]
    return (center.real, center.imag)

def reference(acquisitions, date_pairs):
    intensity = lax.map(date_power, acquisitions)

    def one_pair(indices):
        earlier = acquisitions[indices[0]].astype(jnp.float32)
        later = acquisitions[indices[1]].astype(jnp.float32)
        cross_real = take_looks(earlier[:, 0, :] * later[:, 0, :] + earlier[:, 1, :] * later[:, 1, :])
        cross_imag = take_looks(earlier[:, 1, :] * later[:, 0, :] - earlier[:, 0, :] * later[:, 1, :])
        denominator = jnp.sqrt((intensity[indices[0]] + EPSILON) * (intensity[indices[1]] + EPSILON))
        ratio_real = cross_real / denominator
        ratio_imag = cross_imag / denominator
        magnitude = jnp.sqrt(ratio_real * ratio_real + ratio_imag * ratio_imag).astype(jnp.bfloat16)
        out_real, out_imag = goldstein(ratio_real, ratio_imag)
        return (jnp.stack([out_real, out_imag]).astype(jnp.bfloat16), magnitude)
    filtered, coherence = lax.map(one_pair, jnp.transpose(date_pairs))
    return (filtered, coherence)
```

```python
import math

import jax
import jax.numpy as jnp
import numpy as np
from jax import lax
from jax.experimental import pallas as pl
from jax.experimental.pallas import tpu as pltpu
from jax.sharding import PartitionSpec as P

PATCH = 64
LOOK_AZ = 4
LOOK_RG = 16
HALF = 32
LANES = 128


EPSILON = 1e-06
HIGHEST = lax.Precision.HIGHEST


def fourier_tables(length):
    position = jnp.arange(length, dtype=jnp.int32)
    product = position[:, None] * position[None, :] % length
    angle = product.astype(jnp.float32) * (2.0 * math.pi / length)
    return (jnp.cos(angle), jnp.sin(angle))


def taper_window(length):
    midway = length // 2
    position = jnp.arange(length, dtype=jnp.float32)
    ramp_line = 1.0 - jnp.abs(position + 0.5 - midway) / midway
    return ramp_line[:, None] * ramp_line[None, :]


def transform(real_part, imag_part, cosine_table, sine_table, inverse):
    length = cosine_table.shape[0]
    if inverse:
        matrix = jnp.concatenate(
            [
                jnp.concatenate([cosine_table, sine_table], 1),
                jnp.concatenate([-sine_table, cosine_table], 1),
            ],
            0,
        )
    else:
        matrix = jnp.concatenate(
            [
                jnp.concatenate([cosine_table, -sine_table], 1),
                jnp.concatenate([sine_table, cosine_table], 1),
            ],
            0,
        )
    joined = jnp.concatenate([real_part, imag_part], axis=-1)
    across = jnp.einsum("bnc,cd->bnd", joined, matrix, precision=HIGHEST)
    rotated = jnp.einsum(
        "tkn,bnd->btkd", jnp.stack([cosine_table, sine_table]), across, precision=HIGHEST
    )
    with_cosine = rotated[:, 0]
    with_sine = rotated[:, 1]
    if inverse:
        scaling = 1.0 / (length * length)
        out_real = (with_cosine[..., :length] - with_sine[..., length:]) * scaling
        out_imag = (with_cosine[..., length:] + with_sine[..., :length]) * scaling
    else:
        out_real = with_cosine[..., :length] + with_sine[..., length:]
        out_imag = with_cosine[..., length:] - with_sine[..., :length]
    return (out_real, out_imag)


def goldstein(
    extended_real, extended_imag, cosine_table, sine_table, window, block_lines, block_samples
):
    groups = extended_real.shape[0]
    extent_line = extended_real.shape[1]
    extent_sample = extended_real.shape[2]
    length = cosine_table.shape[0]
    midway = length // 2
    summed_real = jnp.zeros_like(extended_real)
    summed_imag = jnp.zeros_like(extended_imag)
    for start_line in (0, midway):
        for start_sample in (0, midway):
            count_line = (extent_line - start_line) // length
            count_sample = (extent_sample - start_sample) // length
            stop_line = start_line + count_line * length
            stop_sample = start_sample + count_sample * length

            def extract(values):
                region = values[:, start_line:stop_line, start_sample:stop_sample]
                region = region.reshape(groups, count_line, length, count_sample, length)
                return region.transpose(0, 1, 3, 2, 4).reshape(-1, length, length)

            def insert(values):
                shaped = (values * window).reshape(groups, count_line, count_sample, length, length)
                return shaped.transpose(0, 1, 3, 2, 4).reshape(
                    groups, count_line * length, count_sample * length
                )

            spec_real, spec_imag = transform(
                extract(extended_real), extract(extended_imag), cosine_table, sine_table, False
            )
            energy = spec_real * spec_real + spec_imag * spec_imag
            weight = (energy + 1.0) ** 0.25
            weight = weight / jnp.mean(weight, axis=(1, 2), keepdims=True)
            back_real, back_imag = transform(
                spec_real * weight, spec_imag * weight, cosine_table, sine_table, True
            )
            summed_real = summed_real.at[:, start_line:stop_line, start_sample:stop_sample].add(
                insert(back_real)
            )
            summed_imag = summed_imag.at[:, start_line:stop_line, start_sample:stop_sample].add(
                insert(back_imag)
            )
    center_real = summed_real[:, midway : midway + block_lines, midway : midway + block_samples]
    center_imag = summed_imag[:, midway : midway + block_lines, midway : midway + block_samples]
    return (center_real, center_imag)


def local(acquisitions, date_pairs):
    every_pair = lax.all_gather(date_pairs, ("date", "rng", "az"), axis=1, tiled=True)
    by_lines = lax.all_to_all(acquisitions, "date", split_axis=1, concat_axis=0, tiled=True)
    line_count = by_lines.shape[1]
    sample_count = by_lines.shape[3]
    look_lines = line_count // LOOK_AZ
    look_samples = sample_count // LOOK_RG

    def take_looks(values):
        leading = values.shape[:-2]
        shaped = values.reshape(leading + (look_lines, LOOK_AZ, look_samples, LOOK_RG))
        return jnp.sum(shaped, axis=(-3, -1)) * (1.0 / (LOOK_AZ * LOOK_RG))

    real_lines = by_lines[:, :, 0, :].astype(jnp.float32)
    imag_lines = by_lines[:, :, 1, :].astype(jnp.float32)
    intensity = take_looks(real_lines * real_lines + imag_lines * imag_lines)
    pair_total = every_pair.shape[1]
    block_rows = math.gcd(pair_total, 32)
    turns = pair_total // block_rows
    earlier = every_pair[0].reshape(turns, block_rows)
    later = every_pair[1].reshape(turns, block_rows)

    def cross_block(indices):
        left = jnp.take(by_lines, indices[0], axis=0).astype(jnp.float32)
        right = jnp.take(by_lines, indices[1], axis=0).astype(jnp.float32)
        cross_real = take_looks(left[:, :, 0] * right[:, :, 0] + left[:, :, 1] * right[:, :, 1])
        cross_imag = take_looks(left[:, :, 1] * right[:, :, 0] - left[:, :, 0] * right[:, :, 1])
        return (cross_real, cross_imag)

    cross_real, cross_imag = lax.map(cross_block, (earlier, later))
    cross_real = cross_real.reshape(pair_total, look_lines, look_samples)
    cross_imag = cross_imag.reshape(pair_total, look_lines, look_samples)
    power_early = jnp.take(intensity, every_pair[0], axis=0)
    power_late = jnp.take(intensity, every_pair[1], axis=0)
    denominator = jnp.sqrt((power_early + EPSILON) * (power_late + EPSILON))
    payload = jnp.stack([cross_real / denominator, cross_imag / denominator], axis=1)
    partway = lax.all_to_all(
        lax.all_to_all(payload, "date", split_axis=0, concat_axis=2, tiled=True),
        "rng",
        split_axis=0,
        concat_axis=3,
        tiled=True,
    )
    returned = lax.all_to_all(partway, "az", split_axis=0, concat_axis=2, tiled=True)
    ratio_real = returned[:, 0]
    ratio_imag = returned[:, 1]
    coherence = jnp.sqrt(ratio_real * ratio_real + ratio_imag * ratio_imag).astype(jnp.bfloat16)
    block_lines = ratio_real.shape[1]
    block_samples = ratio_real.shape[2]
    padding = ((0, 0), (HALF, HALF), (HALF, HALF))
    extended_real = jnp.pad(ratio_real, padding)
    extended_imag = jnp.pad(ratio_imag, padding)
    cosine_table, sine_table = fourier_tables(PATCH)
    window = taper_window(PATCH)
    out_real, out_imag = goldstein(
        extended_real, extended_imag, cosine_table, sine_table, window, block_lines, block_samples
    )
    filtered = jnp.stack([out_real, out_imag], axis=1).astype(jnp.bfloat16)
    return (filtered, coherence)


def rounded_parts(values):
    high = values.astype(jnp.bfloat16)
    low = (values - high.astype(jnp.float32)).astype(jnp.bfloat16)
    return (high, low)


def split_table(table):
    table = np.asarray(table, np.float32)
    high = table.astype(jnp.bfloat16)
    low = (table - high.astype(np.float32)).astype(jnp.bfloat16)
    return (high, low)


def window_table(cells, samples, columns):
    lane = np.arange(LANES)
    out = np.zeros((cells // samples, LANES, cells), np.float32)
    cell = np.arange(cells)
    per_column = samples // columns
    for line in range(cells // samples):
        out[line] = (lane[:, None] // LOOK_RG == cell[None, :] % per_column) & (
            cell[None, :] // samples == line
        )
    return out.reshape(-1, cells).astype(jnp.bfloat16)


def sample_tables(cells, samples, halves):
    cell = np.arange(cells) % samples
    frequency = np.arange(PATCH)
    forward = []
    place = []
    for half in range(halves):
        position = half * samples + cell
        angle = 2.0 * np.pi * (position[:, None] * frequency[None, :] % PATCH) / PATCH
        forward.append((np.cos(angle), np.sin(angle)))
        place.append(position[:, None] == np.arange(halves * samples)[None, :])
    real = [np.concatenate([c, -s, -s, -c], 1) for c, s in forward]
    imag = [np.concatenate([s, c, c, -s], 1) for c, s in forward]
    return (np.stack(real + imag), np.stack(place).astype(np.float32).astype(jnp.bfloat16))


def line_tables():
    row = np.arange(HALF)
    frequency = np.arange(PATCH)
    angle = 2.0 * np.pi * (frequency[:, None] * row[None, :] % PATCH) / PATCH
    forward = np.concatenate([np.cos(angle), np.sin(angle)], 1)
    ramp = 1.0 - np.abs(np.arange(PATCH) + 0.5 - HALF) / HALF
    first = ramp[:HALF, None]
    second = ramp[HALF:, None]
    cosine = np.cos(angle.T) / PATCH**2
    sine = np.sin(angle.T) / PATCH**2
    flip = (1.0 - 2.0 * (frequency % 2))[None, :]
    top = [second * cosine, second * sine, first * cosine, first * sine]
    bottom = [
        second * flip * cosine,
        second * flip * sine,
        first * cosine,
        first * sine,
    ]
    return (forward, np.stack([np.concatenate(top, 1), np.concatenate(bottom, 1)]))


def back_table(pairs):
    frequency = np.arange(PATCH)
    column = np.arange(HALF)
    angle = 2.0 * np.pi * (frequency[:, None] * column[None, :] % PATCH) / PATCH
    c, s = np.cos(angle), np.sin(angle)
    direct = np.concatenate([np.concatenate([c, s], 1), np.concatenate([-s, c], 1)], 0)
    turned = np.concatenate([np.concatenate([-s, c], 1), np.concatenate([-c, -s], 1)], 0)
    identity = np.eye(pairs)
    return np.concatenate([np.kron(identity, direct), np.kron(identity, turned)], 1)


def dot(left, right):
    return jnp.dot(left, right, preferred_element_type=jnp.float32)


def products_kernel(
    place_ref, pair_ref, own_ref, near_ref, far_ref, last_ref, window_ref,
    out0_ref, out1_ref, out2_ref, out3_ref,
    plain_ref, turned_ref, high_ref, low_ref, sum_ref, root_ref, scale_ref,
):
    group = place_ref[0]
    dates_here = own_ref.shape[0]
    dates = plain_ref.shape[0]
    looks = plain_ref.shape[2]
    pair_total = pair_ref.shape[0] // 2
    even = lax.broadcasted_iota(jnp.int32, (looks, 8, LANES), 1) % 2 == 0
    for offset, ref in enumerate((own_ref, near_ref, far_ref, last_ref)):
        base = (group ^ offset) * dates_here
        for index in range(dates_here):
            values = ref[index].astype(jnp.float32).reshape(looks, 2, 8, LANES)
            for part in range(2):
                lines = values[:, part]
                plain_ref[base + index, part] = lines
                turned_ref[base + index, part] = jnp.where(
                    even, -pltpu.roll(lines, 7, 1), pltpu.roll(lines, 1, 1)
                )

    def keep(slot, first, second):
        joined = jnp.concatenate([first, second], axis=1)
        high, low = rounded_parts(joined)
        for look in range(looks):
            columns = slice(look * LANES, (look + 1) * LANES)
            high_ref[slot, :, columns] = high[look]
            low_ref[slot, :, columns] = low[look]

    def one_pair(index, carry):
        earlier = pair_ref[index]
        later = pair_ref[pair_total + index]
        left0 = plain_ref[earlier, 0]
        left1 = plain_ref[earlier, 1]
        real = left0 * plain_ref[later, 0] + left1 * plain_ref[later, 1]
        imag = left0 * turned_ref[later, 0] + left1 * turned_ref[later, 1]
        keep(index, real, imag)
        return carry

    def two_dates(index, carry):
        def power(date):
            return plain_ref[date, 0] * plain_ref[date, 0] + plain_ref[date, 1] * plain_ref[date, 1]

        keep(pair_total + index, power(2 * index), power(2 * index + 1))
        return carry

    lax.fori_loop(0, dates // 2, two_dates, 0)
    lax.fori_loop(0, pair_total, one_pair, 0)
    rows = high_ref.shape[0] * 16
    width = high_ref.shape[2]
    table = window_ref[...]
    sum_ref[...] = dot(high_ref[...].reshape(rows, width), table) + dot(
        low_ref[...].reshape(rows, width), table
    )
    share = 1.0 / (LOOK_AZ * LOOK_RG)

    def fold(start, count):
        def added(picks):
            total = sum_ref[pl.ds(start * 8 + picks[0], count, stride=8), :]
            for pick in picks[1:]:
                total = total + sum_ref[pl.ds(start * 8 + pick, count, stride=8), :]
            return total

        second = lax.broadcasted_iota(jnp.int32, (count, LANES), 1) // 8 % 2 == 1
        return jnp.where(second, added((2, 3, 6, 7)), added((0, 1, 4, 5))) * share

    root_ref[...] = lax.rsqrt(fold(2 * pair_total, dates) + EPSILON)
    for index in range(pair_total):
        earlier = root_ref[pl.ds(pair_ref[index], 1), :]
        later = root_ref[pl.ds(pair_ref[pair_total + index], 1), :]
        scale_ref[2 * index : 2 * index + 2, :] = jnp.broadcast_to(earlier * later, (2, LANES))
    ratio = fold(0, 2 * pair_total) * scale_ref[...]
    each = ratio.shape[0] // 4
    for index, ref in enumerate((out0_ref, out1_ref, out2_ref, out3_ref)):
        ref[...] = ratio[index * each : (index + 1) * each]


def filter_kernel(
    place_ref, z0_ref, z1_ref, z2_ref, z3_ref, q1_ref, q2_ref, q3_ref,
    sample_high_ref, sample_low_ref, place_table_ref, line_high_ref, line_low_ref,
    back_high_ref, back_low_ref, end_high_ref, end_low_ref,
    filtered_ref, coherence_ref, field_ref, size_ref,
):
    here = place_ref[0]
    pairs = coherence_ref.shape[0]
    rows = 2 * pairs
    lane = lax.broadcasted_iota(jnp.int32, (8, LANES), 1)
    line = lax.broadcasted_iota(jnp.int32, (8, LANES), 0)
    inside = lane // 16 == line
    along = (z0_ref, z1_ref, z2_ref, z3_ref)
    across = (None, q1_ref, q2_ref, q3_ref)
    for far in range(4):
        for near in range(4):
            source = here ^ (4 * far + near)
            core = source & 1
            half = (source >> 1) & 1
            block = core * 4 + (source >> 2)
            if near == 0:
                values = along[far][0:rows, :]
            else:
                values = across[near][far * rows : (far + 1) * rows, :]
            for pair in range(pairs):
                real = values[2 * pair : 2 * pair + 1]
                imag = values[2 * pair + 1 : 2 * pair + 2]
                size = jnp.sqrt(real * real + imag * imag)
                target = pl.ds(pl.multiple_of(pair * PATCH + block * 8, 8), 8)
                field_ref[half, target, :] = jnp.where(
                    inside, jnp.broadcast_to(real, (8, LANES)), 0.0
                )
                field_ref[2 + half, target, :] = jnp.where(
                    inside, jnp.broadcast_to(imag, (8, LANES)), 0.0
                )
                size_ref[half, target, :] = jnp.where(
                    inside, jnp.broadcast_to(size, (8, LANES)), 0.0
                )
    magnitude = dot(size_ref[0].astype(jnp.bfloat16), place_table_ref[0]) + dot(
        size_ref[1].astype(jnp.bfloat16), place_table_ref[1]
    )
    coherence_ref[...] = magnitude.reshape(coherence_ref.shape).astype(coherence_ref.dtype)
    spread = None
    for index in range(4):
        high, low = rounded_parts(field_ref[index])
        table = sample_high_ref[index]
        term = dot(high, table) + dot(low, table) + dot(high, sample_low_ref[index])
        spread = term if spread is None else spread + term
    columns = []
    for half in range(2):
        for pair in range(pairs):
            start = pair * PATCH + half * HALF
            part = spread[start : start + HALF]
            columns.append(jnp.concatenate([part[:, :LANES], part[:, LANES:]], 0))
    high, low = rounded_parts(jnp.concatenate(columns, 1))
    spectrum = (
        dot(line_high_ref[...], high) + dot(line_high_ref[...], low) + dot(line_low_ref[...], high)
    )
    width = pairs * LANES
    top = spectrum[:, :width]
    bottom = spectrum[:, width:]
    sign = 1.0 - 2.0 * (lax.broadcasted_iota(jnp.int32, (PATCH, width), 0) % 2).astype(jnp.float32)
    weighted = []
    for patch in (top, top + sign * bottom, bottom):
        parts = []
        for pair in range(pairs):
            values = patch[:, pair * LANES : (pair + 1) * LANES]
            square = values * values
            energy = square + pltpu.roll(square, LANES // 2, 1)
            weight = lax.rsqrt(lax.rsqrt(energy + 1.0))
            total = jnp.sum(weight, axis=(0, 1), keepdims=True)
            parts.append(values * weight * ((2.0 * PATCH * PATCH) / total))
        weighted.append(jnp.concatenate(parts, 1))
    high, low = rounded_parts(jnp.concatenate(weighted, 0))
    back = dot(high, back_high_ref[...]) + dot(low, back_high_ref[...]) + dot(high, back_low_ref[...])
    pieces = []
    for index in range(3):
        part = back[index * PATCH : (index + 1) * PATCH]
        pieces.append(jnp.concatenate([part[:, :width // 2], part[:, width // 2 :]], 0))
    for half in range(2):
        high, low = rounded_parts(jnp.concatenate([pieces[half], pieces[half + 1]], 0))
        table = end_high_ref[half]
        lines = dot(table, high) + dot(table, low) + dot(end_low_ref[half], high)
        for pair in range(pairs):
            for part in range(2):
                start = (2 * pair + part) * HALF
                filtered_ref[pair, part, half * HALF : (half + 1) * HALF, :] = lines[
                    :, start : start + HALF
                ].astype(filtered_ref.dtype)


def fast_local(acquisitions, date_pairs, sizes):
    depth, across, cores = sizes
    total = depth * across * cores
    dates_here, line_count, _, sample_count = acquisitions.shape
    columns = sample_count // LANES
    lines_each = line_count // depth
    rows = lines_each * columns * 2
    look_lines = lines_each // LOOK_AZ
    look_samples = sample_count // LOOK_RG
    cells = look_lines * look_samples
    pairs_here = date_pairs.shape[1]
    pair_total = pairs_here * total
    dates = dates_here * depth
    group = lax.axis_index("date")
    here = lax.axis_index(("date", "rng", "az"))
    names = ("date", "rng", "az")

    def swap(values, offset):
        return lax.ppermute(values, names, [(i, i ^ offset) for i in range(total)])

    view = acquisitions.reshape(dates_here, line_count, 2, columns, LANES)
    view = view.transpose(0, 1, 3, 2, 4).reshape(dates_here, line_count * columns * 2, LANES)

    def block(offset):
        return lax.dynamic_slice_in_dim(view, (group ^ offset) * rows, rows, 1)

    step = across * cores
    received = {k: swap(block(k), k * step) for k in (3, 2, 1)}
    listed = date_pairs.T[None]
    offset = 1
    while offset < total:
        listed = jnp.concatenate([listed, swap(listed, offset)], 0)
        offset *= 2
    pair_list = listed.reshape(pair_total, 2).T.reshape(-1)
    width = look_lines * LANES
    slots = pair_total + dates // 2
    vmem = pl.BlockSpec(memory_space=pltpu.VMEM)
    smem = pl.BlockSpec(memory_space=pltpu.SMEM)
    piece = jax.ShapeDtypeStruct((2 * pair_total // depth, cells), jnp.float32)
    pieces = pl.pallas_call(
        products_kernel,
        name="products",
        out_shape=[piece] * depth,
        in_specs=[smem, smem] + [vmem] * 5,
        out_specs=[vmem] * depth,
        scratch_shapes=[
            pltpu.VMEM((dates, 2, look_lines, 8, LANES), jnp.float32),
            pltpu.VMEM((dates, 2, look_lines, 8, LANES), jnp.float32),
            pltpu.VMEM((slots, 16, width), jnp.bfloat16),
            pltpu.VMEM((slots, 16, width), jnp.bfloat16),
            pltpu.VMEM((slots * 16, cells), jnp.float32),
            pltpu.VMEM((dates, cells), jnp.float32),
            pltpu.VMEM((2 * pair_total, cells), jnp.float32),
        ],
    )(
        group.reshape(1),
        pair_list,
        block(0),
        received[1],
        received[2],
        received[3],
        jnp.asarray(window_table(cells, look_samples, columns)),
    )
    arrived = [pieces[0]] + [None] * (depth - 1)
    for k in (3, 2, 1):
        arrived[k] = swap(pieces[k], k * step)
    each = 2 * pairs_here
    sideways = []
    for k in (3, 2, 1):
        payload = jnp.concatenate([a[k * each : (k + 1) * each] for a in arrived], 0)
        sideways.append(swap(payload, k))
    sideways = sideways[::-1]
    sample_table, place_table = sample_tables(cells, look_samples, across)
    line_table, end_table = line_tables()
    tables = []
    for table in (sample_table, None, line_table, back_table(pairs_here), end_table):
        tables += [place_table] if table is None else list(split_table(table))
    filtered, coherence = pl.pallas_call(
        filter_kernel,
        name="filter",
        out_shape=[
            jax.ShapeDtypeStruct((pairs_here, 2, PATCH, HALF), jnp.bfloat16),
            jax.ShapeDtypeStruct((pairs_here, PATCH, HALF), jnp.bfloat16),
        ],
        in_specs=[smem] + [vmem] * (depth + 3 + len(tables)),
        out_specs=[vmem, vmem],
        scratch_shapes=[
            pltpu.VMEM((4, pairs_here * PATCH, cells), jnp.float32),
            pltpu.VMEM((2, pairs_here * PATCH, cells), jnp.float32),
        ],
    )(here.reshape(1), *arrived, *sideways, *[jnp.asarray(t) for t in tables])
    return (filtered, coherence)


def fits(acquisitions, date_pairs, sizes):
    depth, across, cores = sizes
    _, line_count, _, sample_count = acquisitions.shape
    look_lines = line_count // depth // LOOK_AZ
    look_samples = sample_count // LOOK_RG
    return (
        sizes == (4, 2, 2)
        and line_count % (depth * LOOK_AZ) == 0
        and sample_count == 2 * LANES
        and look_lines == 8
        and look_lines * look_samples == LANES
        and line_count * cores == LOOK_AZ * PATCH
        and sample_count * across == LOOK_RG * HALF
        and date_pairs.shape[1] == 2
    )


def solution(mesh):
    sizes = tuple(mesh.shape[name] for name in ("date", "rng", "az"))

    def chosen(acquisitions, date_pairs):
        if fits(acquisitions, date_pairs, sizes):
            return fast_local(acquisitions, date_pairs, sizes)
        return local(acquisitions, date_pairs)

    return jax.shard_map(
        chosen,
        mesh=mesh,
        in_specs=(P(("tile", "date"), "az", None, "rng"), P(None, ("date", "rng", "az"))),
        out_specs=(
            P(("tile", "date", "rng", "az"), None, None, None),
            P(("tile", "date", "rng", "az"), None, None),
        ),
        check_vma=False,
    )
```

```python
import math

import jax
import jax.numpy as jnp
import numpy as np
from jax import lax
from jax.experimental import pallas as pl
from jax.experimental.pallas import tpu as pltpu
from jax.sharding import PartitionSpec as P


PATCH = 64
LOOK_AZ = 4
LOOK_RG = 16
HALF = 32
LANES = 128


EPSILON = 1e-06
HIGHEST = lax.Precision.HIGHEST


def fourier_tables(length):
    position = jnp.arange(length, dtype=jnp.int32)
    product = position[:, None] * position[None, :] % length
    angle = product.astype(jnp.float32) * (2.0 * math.pi / length)
    return (jnp.cos(angle), jnp.sin(angle))


def taper_window(length):
    midway = length // 2
    position = jnp.arange(length, dtype=jnp.float32)
    ramp_line = 1.0 - jnp.abs(position + 0.5 - midway) / midway
    return ramp_line[:, None] * ramp_line[None, :]


def transform(real_part, imag_part, cosine_table, sine_table, inverse):
    length = cosine_table.shape[0]
    if inverse:
        matrix = jnp.concatenate(
            [
                jnp.concatenate([cosine_table, sine_table], 1),
                jnp.concatenate([-sine_table, cosine_table], 1),
            ],
            0,
        )
    else:
        matrix = jnp.concatenate(
            [
                jnp.concatenate([cosine_table, -sine_table], 1),
                jnp.concatenate([sine_table, cosine_table], 1),
            ],
            0,
        )
    joined = jnp.concatenate([real_part, imag_part], axis=-1)
    across = jnp.einsum("bnc,cd->bnd", joined, matrix, precision=HIGHEST)
    rotated = jnp.einsum(
        "tkn,bnd->btkd", jnp.stack([cosine_table, sine_table]), across, precision=HIGHEST
    )
    with_cosine = rotated[:, 0]
    with_sine = rotated[:, 1]
    if inverse:
        scaling = 1.0 / (length * length)
        out_real = (with_cosine[..., :length] - with_sine[..., length:]) * scaling
        out_imag = (with_cosine[..., length:] + with_sine[..., :length]) * scaling
    else:
        out_real = with_cosine[..., :length] + with_sine[..., length:]
        out_imag = with_cosine[..., length:] - with_sine[..., :length]
    return (out_real, out_imag)


def goldstein(
    extended_real, extended_imag, cosine_table, sine_table, window, block_lines, block_samples
):
    groups = extended_real.shape[0]
    extent_line = extended_real.shape[1]
    extent_sample = extended_real.shape[2]
    length = cosine_table.shape[0]
    midway = length // 2
    summed_real = jnp.zeros_like(extended_real)
    summed_imag = jnp.zeros_like(extended_imag)
    for start_line in (0, midway):
        for start_sample in (0, midway):
            count_line = (extent_line - start_line) // length
            count_sample = (extent_sample - start_sample) // length
            stop_line = start_line + count_line * length
            stop_sample = start_sample + count_sample * length

            def extract(values):
                region = values[:, start_line:stop_line, start_sample:stop_sample]
                region = region.reshape(groups, count_line, length, count_sample, length)
                return region.transpose(0, 1, 3, 2, 4).reshape(-1, length, length)

            def insert(values):
                shaped = (values * window).reshape(groups, count_line, count_sample, length, length)
                return shaped.transpose(0, 1, 3, 2, 4).reshape(
                    groups, count_line * length, count_sample * length
                )

            spec_real, spec_imag = transform(
                extract(extended_real), extract(extended_imag), cosine_table, sine_table, False
            )
            energy = spec_real * spec_real + spec_imag * spec_imag
            weight = (energy + 1.0) ** 0.25
            weight = weight / jnp.mean(weight, axis=(1, 2), keepdims=True)
            back_real, back_imag = transform(
                spec_real * weight, spec_imag * weight, cosine_table, sine_table, True
            )
            summed_real = summed_real.at[:, start_line:stop_line, start_sample:stop_sample].add(
                insert(back_real)
            )
            summed_imag = summed_imag.at[:, start_line:stop_line, start_sample:stop_sample].add(
                insert(back_imag)
            )
    center_real = summed_real[:, midway : midway + block_lines, midway : midway + block_samples]
    center_imag = summed_imag[:, midway : midway + block_lines, midway : midway + block_samples]
    return (center_real, center_imag)


def local(acquisitions, date_pairs):
    every_pair = lax.all_gather(date_pairs, ("date", "rng", "az"), axis=1, tiled=True)
    by_lines = lax.all_to_all(acquisitions, "date", split_axis=1, concat_axis=0, tiled=True)
    line_count = by_lines.shape[1]
    sample_count = by_lines.shape[3]
    look_lines = line_count // LOOK_AZ
    look_samples = sample_count // LOOK_RG

    def take_looks(values):
        leading = values.shape[:-2]
        shaped = values.reshape(leading + (look_lines, LOOK_AZ, look_samples, LOOK_RG))
        return jnp.sum(shaped, axis=(-3, -1)) * (1.0 / (LOOK_AZ * LOOK_RG))

    real_lines = by_lines[:, :, 0, :].astype(jnp.float32)
    imag_lines = by_lines[:, :, 1, :].astype(jnp.float32)
    intensity = take_looks(real_lines * real_lines + imag_lines * imag_lines)
    pair_total = every_pair.shape[1]
    block_rows = math.gcd(pair_total, 32)
    turns = pair_total // block_rows
    earlier = every_pair[0].reshape(turns, block_rows)
    later = every_pair[1].reshape(turns, block_rows)

    def cross_block(indices):
        left = jnp.take(by_lines, indices[0], axis=0).astype(jnp.float32)
        right = jnp.take(by_lines, indices[1], axis=0).astype(jnp.float32)
        cross_real = take_looks(left[:, :, 0] * right[:, :, 0] + left[:, :, 1] * right[:, :, 1])
        cross_imag = take_looks(left[:, :, 1] * right[:, :, 0] - left[:, :, 0] * right[:, :, 1])
        return (cross_real, cross_imag)

    cross_real, cross_imag = lax.map(cross_block, (earlier, later))
    cross_real = cross_real.reshape(pair_total, look_lines, look_samples)
    cross_imag = cross_imag.reshape(pair_total, look_lines, look_samples)
    power_early = jnp.take(intensity, every_pair[0], axis=0)
    power_late = jnp.take(intensity, every_pair[1], axis=0)
    denominator = jnp.sqrt((power_early + EPSILON) * (power_late + EPSILON))
    payload = jnp.stack([cross_real / denominator, cross_imag / denominator], axis=1)
    partway = lax.all_to_all(
        lax.all_to_all(payload, "date", split_axis=0, concat_axis=2, tiled=True),
        "rng",
        split_axis=0,
        concat_axis=3,
        tiled=True,
    )
    returned = lax.all_to_all(partway, "az", split_axis=0, concat_axis=2, tiled=True)
    ratio_real = returned[:, 0]
    ratio_imag = returned[:, 1]
    coherence = jnp.sqrt(ratio_real * ratio_real + ratio_imag * ratio_imag).astype(jnp.bfloat16)
    block_lines = ratio_real.shape[1]
    block_samples = ratio_real.shape[2]
    padding = ((0, 0), (HALF, HALF), (HALF, HALF))
    extended_real = jnp.pad(ratio_real, padding)
    extended_imag = jnp.pad(ratio_imag, padding)
    cosine_table, sine_table = fourier_tables(PATCH)
    window = taper_window(PATCH)
    out_real, out_imag = goldstein(
        extended_real, extended_imag, cosine_table, sine_table, window, block_lines, block_samples
    )
    filtered = jnp.stack([out_real, out_imag], axis=1).astype(jnp.bfloat16)
    return (filtered, coherence)


def rounded_parts(values):
    high = values.astype(jnp.bfloat16)
    low = (values - high.astype(jnp.float32)).astype(jnp.bfloat16)
    return (high, low)


def split_table(table):
    table = np.asarray(table, np.float32)
    high = table.astype(jnp.bfloat16)
    low = (table - high.astype(np.float32)).astype(jnp.bfloat16)
    return (high, low)


def window_table(cells, samples, columns):
    lane = np.arange(LANES)
    out = np.zeros((cells // samples, LANES, cells), np.float32)
    cell = np.arange(cells)
    per_column = samples // columns
    for line in range(cells // samples):
        out[line] = (lane[:, None] // LOOK_RG == cell[None, :] % per_column) & (
            cell[None, :] // samples == line
        )
    return out.reshape(-1, cells).astype(jnp.bfloat16)


def sample_tables(cells, samples, halves):
    cell = np.arange(cells) % samples
    frequency = np.arange(PATCH)
    forward = []
    place = []
    for half in range(halves):
        position = half * samples + cell
        angle = 2.0 * np.pi * (position[:, None] * frequency[None, :] % PATCH) / PATCH
        forward.append((np.cos(angle), np.sin(angle)))
        place.append(np.arange(halves * samples)[:, None] == position[None, :])
    real = [np.concatenate([c, -s, -s, -c], 1) for c, s in forward]
    imag = [np.concatenate([s, c, c, -s], 1) for c, s in forward]
    return (np.stack(real + imag), np.stack(place).astype(np.float32).astype(jnp.bfloat16))


def line_tables():
    row = np.arange(HALF)
    frequency = np.arange(PATCH)
    angle = 2.0 * np.pi * (frequency[:, None] * row[None, :] % PATCH) / PATCH
    cosine, sine = np.cos(angle), np.sin(angle)
    ramp = 1.0 - np.abs(np.arange(PATCH) + 0.5 - HALF) / HALF
    first, second = ramp[None, :HALF], ramp[None, HALF:]
    flip = (1.0 - 2.0 * (frequency % 2))[:, None]
    none = np.zeros_like(angle)

    def back(wave):
        top = np.concatenate([second * wave, first * wave, none, none], 0)
        bottom = np.concatenate([none, none, second * flip * wave, first * wave], 0)
        return np.concatenate([top, bottom], 1)

    end = np.concatenate([back(cosine), back(sine)], 0) / PATCH**2
    return (np.concatenate([cosine, sine], 1), end)


def back_table(pairs):
    frequency = np.arange(PATCH)
    column = np.arange(HALF)
    angle = 2.0 * np.pi * (column[:, None] * frequency[None, :] % PATCH) / PATCH
    c, s = np.cos(angle), np.sin(angle)
    direct = np.concatenate([np.concatenate([c, -s], 1), np.concatenate([s, c], 1)], 0)
    turned = np.concatenate([np.concatenate([-s, -c], 1), np.concatenate([c, -s], 1)], 0)
    identity = np.eye(pairs)
    return np.concatenate([np.kron(identity, direct), np.kron(identity, turned)], 0)


def dot(left, right):
    return jnp.dot(left, right, preferred_element_type=jnp.float32)


def dot_rows(left, right):
    return lax.dot_general(
        left, right, (((1,), (1,)), ((), ())), preferred_element_type=jnp.float32
    )


def products_kernel(
    place_ref, pair_ref, own_ref, near_ref, far_ref, last_ref, window_ref,
    out0_ref, out1_ref, out2_ref, out3_ref,
    plain_ref, turned_ref, high_ref, low_ref, sum_ref, root_ref, scale_ref,
):
    group = place_ref[0]
    dates_here = own_ref.shape[0]
    dates = plain_ref.shape[0]
    looks = plain_ref.shape[2]
    pair_total = pair_ref.shape[0] // 2
    even = lax.broadcasted_iota(jnp.int32, (looks, 8, LANES), 1) % 2 == 0
    for offset, ref in enumerate((own_ref, near_ref, far_ref, last_ref)):
        base = (group ^ offset) * dates_here
        for index in range(dates_here):
            values = ref[index].astype(jnp.float32).reshape(looks, 2, 8, LANES)
            for part in range(2):
                lines = values[:, part]
                plain_ref[base + index, part] = lines
                turned_ref[base + index, part] = jnp.where(
                    even, -pltpu.roll(lines, 7, 1), pltpu.roll(lines, 1, 1)
                )

    def keep(slot, first, second):
        joined = jnp.concatenate([first, second], axis=1)
        high, low = rounded_parts(joined)
        for look in range(looks):
            columns = slice(look * LANES, (look + 1) * LANES)
            high_ref[slot, :, columns] = high[look]
            low_ref[slot, :, columns] = low[look]

    def one_pair(index, carry):
        earlier = pair_ref[index]
        later = pair_ref[pair_total + index]
        left0 = plain_ref[earlier, 0]
        left1 = plain_ref[earlier, 1]
        real = left0 * plain_ref[later, 0] + left1 * plain_ref[later, 1]
        imag = left0 * turned_ref[later, 0] + left1 * turned_ref[later, 1]
        keep(index, real, imag)
        return carry

    def two_dates(index, carry):
        def power(date):
            return plain_ref[date, 0] * plain_ref[date, 0] + plain_ref[date, 1] * plain_ref[date, 1]

        keep(pair_total + index, power(2 * index), power(2 * index + 1))
        return carry

    lax.fori_loop(0, dates // 2, two_dates, 0)
    lax.fori_loop(0, pair_total, one_pair, 0)
    rows = high_ref.shape[0] * 16
    width = high_ref.shape[2]
    table = window_ref[...]
    sum_ref[...] = dot(high_ref[...].reshape(rows, width), table) + dot(
        low_ref[...].reshape(rows, width), table
    )
    share = 1.0 / (LOOK_AZ * LOOK_RG)

    def fold(start, count):
        def added(picks):
            total = sum_ref[pl.ds(start * 8 + picks[0], count, stride=8), :]
            for pick in picks[1:]:
                total = total + sum_ref[pl.ds(start * 8 + pick, count, stride=8), :]
            return total

        second = lax.broadcasted_iota(jnp.int32, (count, LANES), 1) // 8 % 2 == 1
        return jnp.where(second, added((2, 3, 6, 7)), added((0, 1, 4, 5))) * share

    root_ref[...] = lax.rsqrt(fold(2 * pair_total, dates) + EPSILON)
    for index in range(pair_total):
        earlier = root_ref[pl.ds(pair_ref[index], 1), :]
        later = root_ref[pl.ds(pair_ref[pair_total + index], 1), :]
        scale_ref[2 * index : 2 * index + 2, :] = jnp.broadcast_to(earlier * later, (2, LANES))
    ratio = fold(0, 2 * pair_total) * scale_ref[...]
    each = ratio.shape[0] // 4
    for index, ref in enumerate((out0_ref, out1_ref, out2_ref, out3_ref)):
        ref[...] = ratio[index * each : (index + 1) * each]


def filter_kernel(
    place_ref, z0_ref, z1_ref, z2_ref, z3_ref, q1_ref, q2_ref, q3_ref,
    sample_high_ref, sample_low_ref, place_table_ref, line_high_ref, line_low_ref,
    back_high_ref, back_low_ref, end_high_ref, end_low_ref,
    filtered_ref, coherence_ref, field_ref, size_ref,
):
    here = place_ref[0]
    pairs = coherence_ref.shape[0]
    rows = 2 * pairs
    lane = lax.broadcasted_iota(jnp.int32, (8, LANES), 1)
    line = lax.broadcasted_iota(jnp.int32, (8, LANES), 0)
    inside = lane // 16 == line
    along = (z0_ref, z1_ref, z2_ref, z3_ref)
    across = (None, q1_ref, q2_ref, q3_ref)
    for far in range(4):
        for near in range(4):
            source = here ^ (4 * far + near)
            core = source & 1
            half = (source >> 1) & 1
            block = core * 4 + (source >> 2)
            if near == 0:
                values = along[far][0:rows, :]
            else:
                values = across[near][far * rows : (far + 1) * rows, :]
            for pair in range(pairs):
                real = values[2 * pair : 2 * pair + 1]
                imag = values[2 * pair + 1 : 2 * pair + 2]
                size = jnp.sqrt(real * real + imag * imag)
                target = pl.ds(pl.multiple_of(pair * PATCH + block * 8, 8), 8)
                field_ref[half, target, :] = jnp.where(
                    inside, jnp.broadcast_to(real, (8, LANES)), 0.0
                )
                field_ref[2 + half, target, :] = jnp.where(
                    inside, jnp.broadcast_to(imag, (8, LANES)), 0.0
                )
                size_ref[half, target, :] = jnp.where(
                    inside, jnp.broadcast_to(size, (8, LANES)), 0.0
                )
    for pair in range(pairs):
        lines = slice(pair * PATCH, (pair + 1) * PATCH)
        magnitude = dot_rows(
            place_table_ref[0], size_ref[0, lines].astype(jnp.bfloat16)
        ) + dot_rows(place_table_ref[1], size_ref[1, lines].astype(jnp.bfloat16))
        coherence_ref[pair] = magnitude.astype(coherence_ref.dtype)
    spread = None
    for index in range(4):
        high, low = rounded_parts(field_ref[index])
        table = sample_high_ref[index]
        term = dot(high, table) + dot(low, table) + dot(high, sample_low_ref[index])
        spread = term if spread is None else spread + term
    columns = []
    for half in range(2):
        for pair in range(pairs):
            start = pair * PATCH + half * HALF
            part = spread[start : start + HALF]
            columns.append(jnp.concatenate([part[:, :LANES], part[:, LANES:]], 0))
    high, low = rounded_parts(jnp.concatenate(columns, 1))
    spectrum = (
        dot(line_high_ref[...], high) + dot(line_high_ref[...], low) + dot(line_low_ref[...], high)
    )
    width = pairs * LANES
    top = spectrum[:, :width]
    bottom = spectrum[:, width:]
    sign = 1.0 - 2.0 * (lax.broadcasted_iota(jnp.int32, (PATCH, width), 0) % 2).astype(jnp.float32)
    weighted = []
    for patch in (top, top + sign * bottom, bottom):
        parts = []
        for pair in range(pairs):
            values = patch[:, pair * LANES : (pair + 1) * LANES]
            square = values * values
            energy = square + pltpu.roll(square, LANES // 2, 1)
            weight = lax.rsqrt(lax.rsqrt(energy + 1.0))
            total = jnp.sum(weight, axis=(0, 1), keepdims=True)
            parts.append(values * weight * ((2.0 * PATCH * PATCH) / total))
        weighted.append(jnp.concatenate(parts, 1))
    weighted = [weighted[0], weighted[1], weighted[1], weighted[2]]
    high, low = rounded_parts(jnp.concatenate(weighted, 0))
    back = (
        dot_rows(back_high_ref[...], high)
        + dot_rows(back_high_ref[...], low)
        + dot_rows(back_low_ref[...], high)
    )
    high, low = rounded_parts(jnp.concatenate([back[: width // 2], back[width // 2 :]], 1))
    lines = dot(high, end_high_ref[...]) + dot(low, end_high_ref[...]) + dot(high, end_low_ref[...])
    filtered_ref[...] = lines.reshape(filtered_ref.shape).astype(filtered_ref.dtype)


def fast_local(acquisitions, date_pairs, sizes):
    depth, across, cores = sizes
    total = depth * across * cores
    dates_here, line_count, _, sample_count = acquisitions.shape
    columns = sample_count // LANES
    lines_each = line_count // depth
    rows = lines_each * columns * 2
    look_lines = lines_each // LOOK_AZ
    look_samples = sample_count // LOOK_RG
    cells = look_lines * look_samples
    pairs_here = date_pairs.shape[1]
    pair_total = pairs_here * total
    dates = dates_here * depth
    group = lax.axis_index("date")
    here = lax.axis_index(("date", "rng", "az"))
    names = ("date", "rng", "az")

    def swap(values, offset):
        return lax.ppermute(values, names, [(i, i ^ offset) for i in range(total)])

    view = acquisitions.reshape(dates_here, line_count, 2, columns, LANES)
    view = view.transpose(0, 1, 3, 2, 4).reshape(dates_here, line_count * columns * 2, LANES)

    def block(index):
        return lax.dynamic_slice_in_dim(view, index * rows, rows, 1)

    step = across * cores
    received = {3: swap(block(group ^ 3), 3 * step)}
    listed = date_pairs.T[None]
    listed = jnp.concatenate([listed, swap(listed, 1)], 0)
    late, listed = lax.optimization_barrier((group, listed))
    received[2] = swap(block(late ^ 2), 2 * step)
    received[1] = swap(block(late ^ 1), step)
    own = block(late)
    offset = 2
    while offset < total:
        listed = jnp.concatenate([listed, swap(listed, offset)], 0)
        offset *= 2
    pair_list = listed.reshape(pair_total, 2).T.reshape(-1)
    width = look_lines * LANES
    slots = pair_total + dates // 2
    vmem = pl.BlockSpec(memory_space=pltpu.VMEM)
    smem = pl.BlockSpec(memory_space=pltpu.SMEM)
    piece = jax.ShapeDtypeStruct((2 * pair_total // depth, cells), jnp.float32)
    pieces = pl.pallas_call(
        products_kernel,
        name="products",
        out_shape=[piece] * depth,
        in_specs=[smem, smem] + [vmem] * 5,
        out_specs=[vmem] * depth,
        scratch_shapes=[
            pltpu.VMEM((dates, 2, look_lines, 8, LANES), jnp.float32),
            pltpu.VMEM((dates, 2, look_lines, 8, LANES), jnp.float32),
            pltpu.VMEM((slots, 16, width), jnp.bfloat16),
            pltpu.VMEM((slots, 16, width), jnp.bfloat16),
            pltpu.VMEM((slots * 16, cells), jnp.float32),
            pltpu.VMEM((dates, cells), jnp.float32),
            pltpu.VMEM((2 * pair_total, cells), jnp.float32),
        ],
        compiler_params=pltpu.CompilerParams(vmem_limit_bytes=12 << 20),
    )(
        group.reshape(1),
        pair_list,
        own,
        received[1],
        received[2],
        received[3],
        jnp.asarray(window_table(cells, look_samples, columns)),
    )
    arrived = [pieces[0]] + [None] * (depth - 1)
    for k in (3, 2, 1):
        arrived[k] = swap(pieces[k], k * step)
    each = 2 * pairs_here
    sideways = []
    for k in (3, 2, 1):
        payload = jnp.concatenate([a[k * each : (k + 1) * each] for a in arrived], 0)
        sideways.append(swap(payload, k))
    sideways = sideways[::-1]
    sample_table, place_table = sample_tables(cells, look_samples, across)
    line_table, end_table = line_tables()
    tables = []
    for table in (sample_table, None, line_table, back_table(pairs_here), end_table):
        tables += [place_table] if table is None else list(split_table(table))
    filtered, coherence = pl.pallas_call(
        filter_kernel,
        name="filter",
        out_shape=[
            jax.ShapeDtypeStruct((pairs_here, 2, HALF, PATCH), jnp.bfloat16),
            jax.ShapeDtypeStruct((pairs_here, HALF, PATCH), jnp.bfloat16),
        ],
        in_specs=[smem] + [vmem] * (depth + 3 + len(tables)),
        out_specs=[vmem, vmem],
        scratch_shapes=[
            pltpu.VMEM((4, pairs_here * PATCH, cells), jnp.float32),
            pltpu.VMEM((2, pairs_here * PATCH, cells), jnp.float32),
        ],
        compiler_params=pltpu.CompilerParams(vmem_limit_bytes=8 << 20),
    )(here.reshape(1), *arrived, *sideways, *[jnp.asarray(t) for t in tables])
    return (filtered.transpose(0, 1, 3, 2), coherence.transpose(0, 2, 1))


def fits(acquisitions, date_pairs, sizes):
    depth, across, cores = sizes
    _, line_count, _, sample_count = acquisitions.shape
    look_lines = line_count // depth // LOOK_AZ
    look_samples = sample_count // LOOK_RG
    return (
        sizes == (4, 2, 2)
        and line_count % (depth * LOOK_AZ) == 0
        and sample_count == 2 * LANES
        and look_lines == 8
        and look_lines * look_samples == LANES
        and line_count * cores == LOOK_AZ * PATCH
        and sample_count * across == LOOK_RG * HALF
        and date_pairs.shape[1] == 2
    )


def solution(mesh):
    sizes = tuple(mesh.shape[name] for name in ("date", "rng", "az"))

    def chosen(acquisitions, date_pairs):
        if fits(acquisitions, date_pairs, sizes):
            return fast_local(acquisitions, date_pairs, sizes)
        return local(acquisitions, date_pairs)

    return jax.shard_map(
        chosen,
        mesh=mesh,
        in_specs=(P(("tile", "date"), "az", None, "rng"), P(None, ("date", "rng", "az"))),
        out_specs=(
            P(("tile", "date", "rng", "az"), None, None, None),
            P(("tile", "date", "rng", "az"), None, None),
        ),
        check_vma=False,
    )
```

```python
import math

import jax
import jax.numpy as jnp
import numpy as np
from jax import lax
from jax.experimental import pallas as pl
from jax.experimental.pallas import tpu as pltpu
from jax.sharding import PartitionSpec as P


PATCH = 64
LOOK_AZ = 4
LOOK_RG = 16
HALF = 32
LANES = 128


EPSILON = 1e-06
HIGHEST = lax.Precision.HIGHEST


def fourier_tables(length):
    position = jnp.arange(length, dtype=jnp.int32)
    product = position[:, None] * position[None, :] % length
    angle = product.astype(jnp.float32) * (2.0 * math.pi / length)
    return (jnp.cos(angle), jnp.sin(angle))


def taper_window(length):
    midway = length // 2
    position = jnp.arange(length, dtype=jnp.float32)
    ramp_line = 1.0 - jnp.abs(position + 0.5 - midway) / midway
    return ramp_line[:, None] * ramp_line[None, :]


def transform(real_part, imag_part, cosine_table, sine_table, inverse):
    length = cosine_table.shape[0]
    if inverse:
        matrix = jnp.concatenate(
            [
                jnp.concatenate([cosine_table, sine_table], 1),
                jnp.concatenate([-sine_table, cosine_table], 1),
            ],
            0,
        )
    else:
        matrix = jnp.concatenate(
            [
                jnp.concatenate([cosine_table, -sine_table], 1),
                jnp.concatenate([sine_table, cosine_table], 1),
            ],
            0,
        )
    joined = jnp.concatenate([real_part, imag_part], axis=-1)
    across = jnp.einsum("bnc,cd->bnd", joined, matrix, precision=HIGHEST)
    rotated = jnp.einsum(
        "tkn,bnd->btkd", jnp.stack([cosine_table, sine_table]), across, precision=HIGHEST
    )
    with_cosine = rotated[:, 0]
    with_sine = rotated[:, 1]
    if inverse:
        scaling = 1.0 / (length * length)
        out_real = (with_cosine[..., :length] - with_sine[..., length:]) * scaling
        out_imag = (with_cosine[..., length:] + with_sine[..., :length]) * scaling
    else:
        out_real = with_cosine[..., :length] + with_sine[..., length:]
        out_imag = with_cosine[..., length:] - with_sine[..., :length]
    return (out_real, out_imag)


def goldstein(
    extended_real, extended_imag, cosine_table, sine_table, window, block_lines, block_samples
):
    groups = extended_real.shape[0]
    extent_line = extended_real.shape[1]
    extent_sample = extended_real.shape[2]
    length = cosine_table.shape[0]
    midway = length // 2
    summed_real = jnp.zeros_like(extended_real)
    summed_imag = jnp.zeros_like(extended_imag)
    for start_line in (0, midway):
        for start_sample in (0, midway):
            count_line = (extent_line - start_line) // length
            count_sample = (extent_sample - start_sample) // length
            stop_line = start_line + count_line * length
            stop_sample = start_sample + count_sample * length

            def extract(values):
                region = values[:, start_line:stop_line, start_sample:stop_sample]
                region = region.reshape(groups, count_line, length, count_sample, length)
                return region.transpose(0, 1, 3, 2, 4).reshape(-1, length, length)

            def insert(values):
                shaped = (values * window).reshape(groups, count_line, count_sample, length, length)
                return shaped.transpose(0, 1, 3, 2, 4).reshape(
                    groups, count_line * length, count_sample * length
                )

            spec_real, spec_imag = transform(
                extract(extended_real), extract(extended_imag), cosine_table, sine_table, False
            )
            energy = spec_real * spec_real + spec_imag * spec_imag
            weight = (energy + 1.0) ** 0.25
            weight = weight / jnp.mean(weight, axis=(1, 2), keepdims=True)
            back_real, back_imag = transform(
                spec_real * weight, spec_imag * weight, cosine_table, sine_table, True
            )
            summed_real = summed_real.at[:, start_line:stop_line, start_sample:stop_sample].add(
                insert(back_real)
            )
            summed_imag = summed_imag.at[:, start_line:stop_line, start_sample:stop_sample].add(
                insert(back_imag)
            )
    center_real = summed_real[:, midway : midway + block_lines, midway : midway + block_samples]
    center_imag = summed_imag[:, midway : midway + block_lines, midway : midway + block_samples]
    return (center_real, center_imag)


def local(acquisitions, date_pairs):
    every_pair = lax.all_gather(date_pairs, ("date", "rng", "az"), axis=1, tiled=True)
    by_lines = lax.all_to_all(acquisitions, "date", split_axis=1, concat_axis=0, tiled=True)
    line_count = by_lines.shape[1]
    sample_count = by_lines.shape[3]
    look_lines = line_count // LOOK_AZ
    look_samples = sample_count // LOOK_RG

    def take_looks(values):
        leading = values.shape[:-2]
        shaped = values.reshape(leading + (look_lines, LOOK_AZ, look_samples, LOOK_RG))
        return jnp.sum(shaped, axis=(-3, -1)) * (1.0 / (LOOK_AZ * LOOK_RG))

    real_lines = by_lines[:, :, 0, :].astype(jnp.float32)
    imag_lines = by_lines[:, :, 1, :].astype(jnp.float32)
    intensity = take_looks(real_lines * real_lines + imag_lines * imag_lines)
    pair_total = every_pair.shape[1]
    block_rows = math.gcd(pair_total, 32)
    turns = pair_total // block_rows
    earlier = every_pair[0].reshape(turns, block_rows)
    later = every_pair[1].reshape(turns, block_rows)

    def cross_block(indices):
        left = jnp.take(by_lines, indices[0], axis=0).astype(jnp.float32)
        right = jnp.take(by_lines, indices[1], axis=0).astype(jnp.float32)
        cross_real = take_looks(left[:, :, 0] * right[:, :, 0] + left[:, :, 1] * right[:, :, 1])
        cross_imag = take_looks(left[:, :, 1] * right[:, :, 0] - left[:, :, 0] * right[:, :, 1])
        return (cross_real, cross_imag)

    cross_real, cross_imag = lax.map(cross_block, (earlier, later))
    cross_real = cross_real.reshape(pair_total, look_lines, look_samples)
    cross_imag = cross_imag.reshape(pair_total, look_lines, look_samples)
    power_early = jnp.take(intensity, every_pair[0], axis=0)
    power_late = jnp.take(intensity, every_pair[1], axis=0)
    denominator = jnp.sqrt((power_early + EPSILON) * (power_late + EPSILON))
    payload = jnp.stack([cross_real / denominator, cross_imag / denominator], axis=1)
    partway = lax.all_to_all(
        lax.all_to_all(payload, "date", split_axis=0, concat_axis=2, tiled=True),
        "rng",
        split_axis=0,
        concat_axis=3,
        tiled=True,
    )
    returned = lax.all_to_all(partway, "az", split_axis=0, concat_axis=2, tiled=True)
    ratio_real = returned[:, 0]
    ratio_imag = returned[:, 1]
    coherence = jnp.sqrt(ratio_real * ratio_real + ratio_imag * ratio_imag).astype(jnp.bfloat16)
    block_lines = ratio_real.shape[1]
    block_samples = ratio_real.shape[2]
    padding = ((0, 0), (HALF, HALF), (HALF, HALF))
    extended_real = jnp.pad(ratio_real, padding)
    extended_imag = jnp.pad(ratio_imag, padding)
    cosine_table, sine_table = fourier_tables(PATCH)
    window = taper_window(PATCH)
    out_real, out_imag = goldstein(
        extended_real, extended_imag, cosine_table, sine_table, window, block_lines, block_samples
    )
    filtered = jnp.stack([out_real, out_imag], axis=1).astype(jnp.bfloat16)
    return (filtered, coherence)


def rounded_parts(values):
    high = values.astype(jnp.bfloat16)
    low = (values - high.astype(jnp.float32)).astype(jnp.bfloat16)
    return (high, low)


def split_table(table):
    table = np.asarray(table, np.float32)
    high = table.astype(jnp.bfloat16)
    low = (table - high.astype(np.float32)).astype(jnp.bfloat16)
    return (high, low)


def window_table(cells, samples, columns):
    lane = np.arange(LANES)
    out = np.zeros((cells // samples, LANES, cells), np.float32)
    cell = np.arange(cells)
    per_column = samples // columns
    for line in range(cells // samples):
        out[line] = (lane[:, None] // LOOK_RG == cell[None, :] % per_column) & (
            cell[None, :] // samples == line
        )
    return out.reshape(-1, cells).astype(jnp.bfloat16)


def sample_tables(cells, samples, halves):
    cell = np.arange(cells) % samples
    frequency = np.arange(PATCH)
    forward = []
    place = []
    for half in range(halves):
        position = half * samples + cell
        angle = 2.0 * np.pi * (position[:, None] * frequency[None, :] % PATCH) / PATCH
        forward.append((np.cos(angle), np.sin(angle)))
        place.append(np.arange(halves * samples)[:, None] == position[None, :])
    real = [np.concatenate([c, -s, -s, -c], 1) for c, s in forward]
    imag = [np.concatenate([s, c, c, -s], 1) for c, s in forward]
    return (np.stack(real + imag), np.stack(place).astype(np.float32).astype(jnp.bfloat16))


def line_tables():
    row = np.arange(HALF)
    frequency = np.arange(PATCH)
    angle = 2.0 * np.pi * (frequency[:, None] * row[None, :] % PATCH) / PATCH
    cosine, sine = np.cos(angle), np.sin(angle)
    ramp = 1.0 - np.abs(np.arange(PATCH) + 0.5 - HALF) / HALF
    first, second = ramp[None, :HALF], ramp[None, HALF:]
    flip = (1.0 - 2.0 * (frequency % 2))[:, None]
    none = np.zeros_like(angle)

    def back(wave):
        top = np.concatenate([second * wave, first * wave, none, none], 0)
        bottom = np.concatenate([none, none, second * flip * wave, first * wave], 0)
        return np.concatenate([top, bottom], 1)

    end = np.concatenate([back(cosine), back(sine)], 0) / PATCH**2
    return (np.concatenate([cosine, sine], 1), end)


def back_table(pairs):
    frequency = np.arange(PATCH)
    column = np.arange(HALF)
    angle = 2.0 * np.pi * (column[:, None] * frequency[None, :] % PATCH) / PATCH
    c, s = np.cos(angle), np.sin(angle)
    direct = np.concatenate([np.concatenate([c, -s], 1), np.concatenate([s, c], 1)], 0)
    turned = np.concatenate([np.concatenate([-s, -c], 1), np.concatenate([c, -s], 1)], 0)
    identity = np.eye(pairs)
    return np.concatenate([np.kron(identity, direct), np.kron(identity, turned)], 0)


def dot(left, right):
    return jnp.dot(left, right, preferred_element_type=jnp.float32)


def dot_rows(left, right):
    return lax.dot_general(
        left, right, (((1,), (1,)), ((), ())), preferred_element_type=jnp.float32
    )


def products_kernel(
    place_ref, pair_ref, own_ref, near_ref, far_ref, last_ref, window_ref,
    out_ref,
    plain_ref, turned_ref, high_ref, low_ref, sum_ref, root_ref, scale_ref,
):
    group = place_ref[0]
    dates_here = own_ref.shape[0]
    dates = plain_ref.shape[0]
    looks = plain_ref.shape[2]
    owners = pair_ref.shape[0]
    pairs_here = pair_ref.shape[1] // 2
    pair_total = owners * pairs_here
    even = lax.broadcasted_iota(jnp.int32, (looks, 8, LANES), 1) % 2 == 0
    for offset, ref in enumerate((own_ref, near_ref, far_ref, last_ref)):
        base = (group ^ offset) * dates_here
        for index in range(dates_here):
            values = ref[index].astype(jnp.float32).reshape(looks, 2, 8, LANES)
            for part in range(2):
                lines = values[:, part]
                plain_ref[base + index, part] = lines
                turned_ref[base + index, part] = jnp.where(
                    even, -pltpu.roll(lines, 7, 1), pltpu.roll(lines, 1, 1)
                )

    def keep(slot, first, second):
        joined = jnp.concatenate([first, second], axis=1)
        high, low = rounded_parts(joined)
        for look in range(looks):
            columns = slice(look * LANES, (look + 1) * LANES)
            high_ref[slot, :, columns] = high[look]
            low_ref[slot, :, columns] = low[look]

    def one_pair(index, carry):
        owner = index // pairs_here
        earlier = pair_ref[owner, index % pairs_here]
        later = pair_ref[owner, pairs_here + index % pairs_here]
        left0 = plain_ref[earlier, 0]
        left1 = plain_ref[earlier, 1]
        real = left0 * plain_ref[later, 0] + left1 * plain_ref[later, 1]
        imag = left0 * turned_ref[later, 0] + left1 * turned_ref[later, 1]
        keep(index, real, imag)
        return carry

    def two_dates(index, carry):
        def power(date):
            return plain_ref[date, 0] * plain_ref[date, 0] + plain_ref[date, 1] * plain_ref[date, 1]

        keep(pair_total + index, power(2 * index), power(2 * index + 1))
        return carry

    lax.fori_loop(0, dates // 2, two_dates, 0)
    lax.fori_loop(0, pair_total, one_pair, 0)
    rows = high_ref.shape[0] * 16
    width = high_ref.shape[2]
    table = window_ref[...]
    sum_ref[...] = dot(high_ref[...].reshape(rows, width), table) + dot(
        low_ref[...].reshape(rows, width), table
    )
    share = 1.0 / (LOOK_AZ * LOOK_RG)

    def fold(start, count):
        def added(picks):
            total = sum_ref[pl.ds(start * 8 + picks[0], count, stride=8), :]
            for pick in picks[1:]:
                total = total + sum_ref[pl.ds(start * 8 + pick, count, stride=8), :]
            return total

        second = lax.broadcasted_iota(jnp.int32, (count, LANES), 1) // 8 % 2 == 1
        return jnp.where(second, added((2, 3, 6, 7)), added((0, 1, 4, 5))) * share

    root_ref[...] = lax.rsqrt(fold(2 * pair_total, dates) + EPSILON)
    for owner in range(owners):
        for index in range(pairs_here):
            earlier = root_ref[pl.ds(pair_ref[owner, index], 1), :]
            later = root_ref[pl.ds(pair_ref[owner, pairs_here + index], 1), :]
            start = 2 * (owner * pairs_here + index)
            scale_ref[start : start + 2, :] = jnp.broadcast_to(earlier * later, (2, LANES))
    ratio = fold(0, 2 * pair_total) * scale_ref[...]
    out_ref[...] = ratio.reshape(out_ref.shape)


def filter_kernel(
    ratio_ref, sample_high_ref, sample_low_ref, place_table_ref, line_high_ref, line_low_ref,
    back_high_ref, back_low_ref, end_high_ref, end_low_ref,
    filtered_ref, coherence_ref, field_ref, size_ref,
):
    pairs = coherence_ref.shape[0]
    lane = lax.broadcasted_iota(jnp.int32, (8, LANES), 1)
    line = lax.broadcasted_iota(jnp.int32, (8, LANES), 0)
    inside = lane // 16 == line
    for source in range(ratio_ref.shape[0]):
        core = source & 1
        half = (source >> 1) & 1
        block = core * 4 + (source >> 2)
        values = ratio_ref[source]
        for pair in range(pairs):
            real = values[2 * pair : 2 * pair + 1]
            imag = values[2 * pair + 1 : 2 * pair + 2]
            size = jnp.sqrt(real * real + imag * imag)
            start = pair * PATCH + block * 8
            for target, index, row in (
                (field_ref, half, real),
                (field_ref, 2 + half, imag),
                (size_ref, half, size),
            ):
                target[index, start : start + 8, :] = jnp.where(
                    inside, jnp.broadcast_to(row, (8, LANES)), 0.0
                )
    for pair in range(pairs):
        lines = slice(pair * PATCH, (pair + 1) * PATCH)
        magnitude = dot_rows(
            place_table_ref[0], size_ref[0, lines].astype(jnp.bfloat16)
        ) + dot_rows(place_table_ref[1], size_ref[1, lines].astype(jnp.bfloat16))
        coherence_ref[pair] = magnitude.astype(coherence_ref.dtype)
    spread = None
    for index in range(4):
        high, low = rounded_parts(field_ref[index])
        table = sample_high_ref[index]
        term = dot(high, table) + dot(low, table) + dot(high, sample_low_ref[index])
        spread = term if spread is None else spread + term
    columns = []
    for half in range(2):
        for pair in range(pairs):
            start = pair * PATCH + half * HALF
            part = spread[start : start + HALF]
            columns.append(jnp.concatenate([part[:, :LANES], part[:, LANES:]], 0))
    high, low = rounded_parts(jnp.concatenate(columns, 1))
    spectrum = (
        dot(line_high_ref[...], high) + dot(line_high_ref[...], low) + dot(line_low_ref[...], high)
    )
    width = pairs * LANES
    top = spectrum[:, :width]
    bottom = spectrum[:, width:]
    sign = 1.0 - 2.0 * (lax.broadcasted_iota(jnp.int32, (PATCH, width), 0) % 2).astype(jnp.float32)
    weighted = []
    for patch in (top, top + sign * bottom, bottom):
        parts = []
        for pair in range(pairs):
            values = patch[:, pair * LANES : (pair + 1) * LANES]
            square = values * values
            energy = square + pltpu.roll(square, LANES // 2, 1)
            weight = lax.rsqrt(lax.rsqrt(energy + 1.0))
            total = jnp.sum(weight, axis=(0, 1), keepdims=True)
            parts.append(values * weight * ((2.0 * PATCH * PATCH) / total))
        weighted.append(jnp.concatenate(parts, 1))
    weighted = [weighted[0], weighted[1], weighted[1], weighted[2]]
    high, low = rounded_parts(jnp.concatenate(weighted, 0))
    back = (
        dot_rows(back_high_ref[...], high)
        + dot_rows(back_high_ref[...], low)
        + dot_rows(back_low_ref[...], high)
    )
    high, low = rounded_parts(jnp.concatenate([back[: width // 2], back[width // 2 :]], 1))
    lines = dot(high, end_high_ref[...]) + dot(low, end_high_ref[...]) + dot(high, end_low_ref[...])
    filtered_ref[...] = lines.reshape(filtered_ref.shape).astype(filtered_ref.dtype)


def fast_local(acquisitions, date_pairs, sizes):
    depth, across, cores = sizes
    total = depth * across * cores
    dates_here, line_count, _, sample_count = acquisitions.shape
    columns = sample_count // LANES
    lines_each = line_count // depth
    rows = lines_each * columns * 2
    look_lines = lines_each // LOOK_AZ
    look_samples = sample_count // LOOK_RG
    cells = look_lines * look_samples
    pairs_here = date_pairs.shape[1]
    pair_total = pairs_here * total
    dates = dates_here * depth
    group = lax.axis_index("date")
    names = ("date", "rng", "az")

    def swap(values, offset):
        return lax.ppermute(values, names, [(i, i ^ offset) for i in range(total)])

    view = acquisitions.reshape(dates_here, line_count, 2, columns, LANES)
    view = view.transpose(0, 1, 3, 2, 4).reshape(dates_here, line_count * columns * 2, LANES)

    def block(source, offset):
        return lax.dynamic_slice_in_dim(source, (group ^ offset) * rows, rows, 1)

    step = across * cores
    farthest, rest = lax.optimization_barrier((block(view, 3), view))
    received = {3: swap(farthest, 3 * step)}
    for offset in (1, 2):
        received[offset] = swap(block(rest, offset), offset * step)
    own = block(rest, 0)
    listed = jnp.broadcast_to(date_pairs.reshape(1, -1), (total, 2 * pairs_here))
    pair_list = lax.all_to_all(listed, names, 0, 0, tiled=True)
    width = look_lines * LANES
    slots = pair_total + dates // 2
    vmem = pl.BlockSpec(memory_space=pltpu.VMEM)
    smem = pl.BlockSpec(memory_space=pltpu.SMEM)
    ratios = pl.pallas_call(
        products_kernel,
        name="products",
        out_shape=jax.ShapeDtypeStruct((total, 2 * pairs_here, cells), jnp.float32),
        in_specs=[smem, smem] + [vmem] * 5,
        out_specs=vmem,
        scratch_shapes=[
            pltpu.VMEM((dates, 2, look_lines, 8, LANES), jnp.float32),
            pltpu.VMEM((dates, 2, look_lines, 8, LANES), jnp.float32),
            pltpu.VMEM((slots, 16, width), jnp.bfloat16),
            pltpu.VMEM((slots, 16, width), jnp.bfloat16),
            pltpu.VMEM((slots * 16, cells), jnp.float32),
            pltpu.VMEM((dates, cells), jnp.float32),
            pltpu.VMEM((2 * pair_total, cells), jnp.float32),
        ],
        compiler_params=pltpu.CompilerParams(vmem_limit_bytes=12 << 20),
    )(
        group.reshape(1),
        pair_list,
        own,
        received[1],
        received[2],
        received[3],
        jnp.asarray(window_table(cells, look_samples, columns)),
    )
    arrived = lax.all_to_all(ratios, names, 0, 0, tiled=True)
    sample_table, place_table = sample_tables(cells, look_samples, across)
    line_table, end_table = line_tables()
    tables = []
    for table in (sample_table, None, line_table, back_table(pairs_here), end_table):
        tables += [place_table] if table is None else list(split_table(table))
    filtered, coherence = pl.pallas_call(
        filter_kernel,
        name="filter",
        out_shape=[
            jax.ShapeDtypeStruct((pairs_here, 2, HALF, PATCH), jnp.bfloat16),
            jax.ShapeDtypeStruct((pairs_here, HALF, PATCH), jnp.bfloat16),
        ],
        in_specs=[vmem] * (1 + len(tables)),
        out_specs=[vmem, vmem],
        scratch_shapes=[
            pltpu.VMEM((4, pairs_here * PATCH, cells), jnp.float32),
            pltpu.VMEM((2, pairs_here * PATCH, cells), jnp.float32),
        ],
        compiler_params=pltpu.CompilerParams(vmem_limit_bytes=8 << 20),
    )(arrived, *[jnp.asarray(t) for t in tables])
    return (filtered.transpose(0, 1, 3, 2), coherence.transpose(0, 2, 1))


def fits(acquisitions, date_pairs, sizes):
    depth, across, cores = sizes
    _, line_count, _, sample_count = acquisitions.shape
    look_lines = line_count // depth // LOOK_AZ
    look_samples = sample_count // LOOK_RG
    return (
        sizes == (4, 2, 2)
        and line_count % (depth * LOOK_AZ) == 0
        and sample_count == 2 * LANES
        and look_lines == 8
        and look_lines * look_samples == LANES
        and line_count * cores == LOOK_AZ * PATCH
        and sample_count * across == LOOK_RG * HALF
        and date_pairs.shape[1] == 2
    )


def solution(mesh):
    sizes = tuple(mesh.shape[name] for name in ("date", "rng", "az"))

    def chosen(acquisitions, date_pairs):
        if fits(acquisitions, date_pairs, sizes):
            return fast_local(acquisitions, date_pairs, sizes)
        return local(acquisitions, date_pairs)

    return jax.shard_map(
        chosen,
        mesh=mesh,
        in_specs=(P(("tile", "date"), "az", None, "rng"), P(None, ("date", "rng", "az"))),
        out_specs=(
            P(("tile", "date", "rng", "az"), None, None, None),
            P(("tile", "date", "rng", "az"), None, None),
        ),
        check_vma=False,
    )
```

```python
import math

import jax
import jax.numpy as jnp
import numpy as np
from jax import lax
from jax.experimental import pallas as pl
from jax.experimental.pallas import tpu as pltpu
from jax.sharding import PartitionSpec as P


PATCH = 64
LOOK_AZ = 4
LOOK_RG = 16
HALF = 32
LANES = 128


EPSILON = 1e-06
HIGHEST = lax.Precision.HIGHEST


def fourier_tables(length):
    position = jnp.arange(length, dtype=jnp.int32)
    product = position[:, None] * position[None, :] % length
    angle = product.astype(jnp.float32) * (2.0 * math.pi / length)
    return (jnp.cos(angle), jnp.sin(angle))


def taper_window(length):
    midway = length // 2
    position = jnp.arange(length, dtype=jnp.float32)
    ramp_line = 1.0 - jnp.abs(position + 0.5 - midway) / midway
    return ramp_line[:, None] * ramp_line[None, :]


def transform(real_part, imag_part, cosine_table, sine_table, inverse):
    length = cosine_table.shape[0]
    if inverse:
        matrix = jnp.concatenate(
            [
                jnp.concatenate([cosine_table, sine_table], 1),
                jnp.concatenate([-sine_table, cosine_table], 1),
            ],
            0,
        )
    else:
        matrix = jnp.concatenate(
            [
                jnp.concatenate([cosine_table, -sine_table], 1),
                jnp.concatenate([sine_table, cosine_table], 1),
            ],
            0,
        )
    joined = jnp.concatenate([real_part, imag_part], axis=-1)
    across = jnp.einsum("bnc,cd->bnd", joined, matrix, precision=HIGHEST)
    rotated = jnp.einsum(
        "tkn,bnd->btkd", jnp.stack([cosine_table, sine_table]), across, precision=HIGHEST
    )
    with_cosine = rotated[:, 0]
    with_sine = rotated[:, 1]
    if inverse:
        scaling = 1.0 / (length * length)
        out_real = (with_cosine[..., :length] - with_sine[..., length:]) * scaling
        out_imag = (with_cosine[..., length:] + with_sine[..., :length]) * scaling
    else:
        out_real = with_cosine[..., :length] + with_sine[..., length:]
        out_imag = with_cosine[..., length:] - with_sine[..., :length]
    return (out_real, out_imag)


def goldstein(
    extended_real, extended_imag, cosine_table, sine_table, window, block_lines, block_samples
):
    groups = extended_real.shape[0]
    extent_line = extended_real.shape[1]
    extent_sample = extended_real.shape[2]
    length = cosine_table.shape[0]
    midway = length // 2
    summed_real = jnp.zeros_like(extended_real)
    summed_imag = jnp.zeros_like(extended_imag)
    for start_line in (0, midway):
        for start_sample in (0, midway):
            count_line = (extent_line - start_line) // length
            count_sample = (extent_sample - start_sample) // length
            stop_line = start_line + count_line * length
            stop_sample = start_sample + count_sample * length

            def extract(values):
                region = values[:, start_line:stop_line, start_sample:stop_sample]
                region = region.reshape(groups, count_line, length, count_sample, length)
                return region.transpose(0, 1, 3, 2, 4).reshape(-1, length, length)

            def insert(values):
                shaped = (values * window).reshape(groups, count_line, count_sample, length, length)
                return shaped.transpose(0, 1, 3, 2, 4).reshape(
                    groups, count_line * length, count_sample * length
                )

            spec_real, spec_imag = transform(
                extract(extended_real), extract(extended_imag), cosine_table, sine_table, False
            )
            energy = spec_real * spec_real + spec_imag * spec_imag
            weight = (energy + 1.0) ** 0.25
            weight = weight / jnp.mean(weight, axis=(1, 2), keepdims=True)
            back_real, back_imag = transform(
                spec_real * weight, spec_imag * weight, cosine_table, sine_table, True
            )
            summed_real = summed_real.at[:, start_line:stop_line, start_sample:stop_sample].add(
                insert(back_real)
            )
            summed_imag = summed_imag.at[:, start_line:stop_line, start_sample:stop_sample].add(
                insert(back_imag)
            )
    center_real = summed_real[:, midway : midway + block_lines, midway : midway + block_samples]
    center_imag = summed_imag[:, midway : midway + block_lines, midway : midway + block_samples]
    return (center_real, center_imag)


def local(acquisitions, date_pairs):
    every_pair = lax.all_gather(date_pairs, ("date", "rng", "az"), axis=1, tiled=True)
    by_lines = lax.all_to_all(acquisitions, "date", split_axis=1, concat_axis=0, tiled=True)
    line_count = by_lines.shape[1]
    sample_count = by_lines.shape[3]
    look_lines = line_count // LOOK_AZ
    look_samples = sample_count // LOOK_RG

    def take_looks(values):
        leading = values.shape[:-2]
        shaped = values.reshape(leading + (look_lines, LOOK_AZ, look_samples, LOOK_RG))
        return jnp.sum(shaped, axis=(-3, -1)) * (1.0 / (LOOK_AZ * LOOK_RG))

    real_lines = by_lines[:, :, 0, :].astype(jnp.float32)
    imag_lines = by_lines[:, :, 1, :].astype(jnp.float32)
    intensity = take_looks(real_lines * real_lines + imag_lines * imag_lines)
    pair_total = every_pair.shape[1]
    block_rows = math.gcd(pair_total, 32)
    turns = pair_total // block_rows
    earlier = every_pair[0].reshape(turns, block_rows)
    later = every_pair[1].reshape(turns, block_rows)

    def cross_block(indices):
        left = jnp.take(by_lines, indices[0], axis=0).astype(jnp.float32)
        right = jnp.take(by_lines, indices[1], axis=0).astype(jnp.float32)
        cross_real = take_looks(left[:, :, 0] * right[:, :, 0] + left[:, :, 1] * right[:, :, 1])
        cross_imag = take_looks(left[:, :, 1] * right[:, :, 0] - left[:, :, 0] * right[:, :, 1])
        return (cross_real, cross_imag)

    cross_real, cross_imag = lax.map(cross_block, (earlier, later))
    cross_real = cross_real.reshape(pair_total, look_lines, look_samples)
    cross_imag = cross_imag.reshape(pair_total, look_lines, look_samples)
    power_early = jnp.take(intensity, every_pair[0], axis=0)
    power_late = jnp.take(intensity, every_pair[1], axis=0)
    denominator = jnp.sqrt((power_early + EPSILON) * (power_late + EPSILON))
    payload = jnp.stack([cross_real / denominator, cross_imag / denominator], axis=1)
    partway = lax.all_to_all(
        lax.all_to_all(payload, "date", split_axis=0, concat_axis=2, tiled=True),
        "rng",
        split_axis=0,
        concat_axis=3,
        tiled=True,
    )
    returned = lax.all_to_all(partway, "az", split_axis=0, concat_axis=2, tiled=True)
    ratio_real = returned[:, 0]
    ratio_imag = returned[:, 1]
    coherence = jnp.sqrt(ratio_real * ratio_real + ratio_imag * ratio_imag).astype(jnp.bfloat16)
    block_lines = ratio_real.shape[1]
    block_samples = ratio_real.shape[2]
    padding = ((0, 0), (HALF, HALF), (HALF, HALF))
    extended_real = jnp.pad(ratio_real, padding)
    extended_imag = jnp.pad(ratio_imag, padding)
    cosine_table, sine_table = fourier_tables(PATCH)
    window = taper_window(PATCH)
    out_real, out_imag = goldstein(
        extended_real, extended_imag, cosine_table, sine_table, window, block_lines, block_samples
    )
    filtered = jnp.stack([out_real, out_imag], axis=1).astype(jnp.bfloat16)
    return (filtered, coherence)


def rounded_parts(values):
    high = values.astype(jnp.bfloat16)
    low = (values - high.astype(jnp.float32)).astype(jnp.bfloat16)
    return (high, low)


def split_table(table):
    table = np.asarray(table, np.float32)
    high = table.astype(jnp.bfloat16)
    low = (table - high.astype(np.float32)).astype(jnp.bfloat16)
    return (high, low)


def window_table(cells):
    lane = np.arange(LANES)
    table = lane[:, None] // LOOK_RG == np.arange(cells)[None, :] % (LANES // LOOK_RG)
    return np.concatenate([table, table], 0).astype(np.float32).astype(jnp.bfloat16)


def sample_tables(cells, samples, halves):
    cell = np.arange(cells) % samples
    frequency = np.arange(PATCH)
    forward = []
    place = []
    for half in range(halves):
        position = half * samples + cell
        angle = 2.0 * np.pi * (position[:, None] * frequency[None, :] % PATCH) / PATCH
        forward.append((np.cos(angle), np.sin(angle)))
        place.append(np.arange(halves * samples)[:, None] == position[None, :])
    real = [np.concatenate([c, -s, -s, -c], 1) for c, s in forward]
    imag = [np.concatenate([s, c, c, -s], 1) for c, s in forward]
    return (
        np.concatenate(real + imag, 0),
        np.concatenate(place, 1).astype(np.float32).astype(jnp.bfloat16),
    )


def line_tables():
    row = np.arange(HALF)
    frequency = np.arange(PATCH)
    angle = 2.0 * np.pi * (frequency[:, None] * row[None, :] % PATCH) / PATCH
    cosine, sine = np.cos(angle), np.sin(angle)
    ramp = 1.0 - np.abs(np.arange(PATCH) + 0.5 - HALF) / HALF
    first, second = ramp[None, :HALF], ramp[None, HALF:]
    flip = (1.0 - 2.0 * (frequency % 2))[:, None]
    none = np.zeros_like(angle)

    def back(wave):
        top = np.concatenate([second * wave, first * wave, none, none], 0)
        bottom = np.concatenate([none, none, second * flip * wave, first * wave], 0)
        return np.concatenate([top, bottom], 1)

    end = np.concatenate([back(cosine), back(sine)], 0) / PATCH**2
    return (np.concatenate([cosine, sine], 1), end)


def back_table(pairs):
    frequency = np.arange(PATCH)
    column = np.arange(HALF)
    angle = 2.0 * np.pi * (column[:, None] * frequency[None, :] % PATCH) / PATCH
    c, s = np.cos(angle), np.sin(angle)
    direct = np.concatenate([np.concatenate([c, -s], 1), np.concatenate([s, c], 1)], 0)
    turned = np.concatenate([np.concatenate([-s, -c], 1), np.concatenate([c, -s], 1)], 0)
    identity = np.eye(pairs)
    return np.concatenate([np.kron(identity, direct), np.kron(identity, turned)], 0)


def dot(left, right):
    return jnp.dot(left, right, preferred_element_type=jnp.float32)


def dot_rows(left, right):
    return lax.dot_general(
        left, right, (((1,), (1,)), ((), ())), preferred_element_type=jnp.float32
    )


def products_kernel(
    place_ref, pair_ref, own_ref, near_ref, far_ref, last_ref, window_ref,
    out_ref,
    part_ref, split_ref, power_ref, sum_ref, date_ref, root_ref, scale_ref,
):
    group = place_ref[0]
    dates_here = own_ref.shape[0]
    dates = part_ref.shape[0]
    owners = pair_ref.shape[0]
    pairs_here = pair_ref.shape[1] // 2
    pair_total = owners * pairs_here
    row = lax.broadcasted_iota(jnp.int32, (8, LANES), 0)
    low = row < 4
    even = row % 2 == 0

    def split(target, slot, first, second):
        high, rest = rounded_parts(jnp.concatenate([first, second], axis=0))
        target[slot, :, :LANES] = high
        target[slot, :, LANES:] = rest

    def total(terms):
        while len(terms) > 1:
            terms = [a + b for a, b in zip(terms[::2], terms[1::2])]
        return terms[0]

    for offset, ref in enumerate((own_ref, near_ref, far_ref, last_ref)):
        base = (group ^ offset) * dates_here
        for index in range(dates_here):
            values = ref[index].astype(jnp.float32).reshape(8, 2, 8, LANES)
            for pick in range(2):
                squares = []
                for part in range(2):
                    lines = []
                    for look in (pick, pick + 2):
                        upper, lower = values[look, part], values[look + 4, part]
                        lines.append(
                            (
                                jnp.where(low, upper, pltpu.roll(lower, 4, 0)),
                                jnp.where(low, pltpu.roll(upper, 4, 0), lower),
                            )
                        )
                    for line in range(2):
                        first, second = lines[0][line], lines[1][line]
                        real = jnp.where(even, first, pltpu.roll(second, 1, 0))
                        imag = jnp.where(even, pltpu.roll(first, 7, 0), second)
                        part_ref[base + index, 0, pick, 2 * part + line] = real
                        part_ref[base + index, 1, pick, 2 * part + line] = imag
                        squares += [real * real, imag * imag]
                high, rest = rounded_parts(total(squares))
                power_ref[base + index, 8 * pick : 8 * pick + 8, :LANES] = high
                power_ref[base + index, 8 * pick : 8 * pick + 8, LANES:] = rest

    def one_owner(owner, carry):
        for index in range(pairs_here):
            earlier = pair_ref[owner, index]
            later = pair_ref[owner, pairs_here + index]
            real, imag = [], []
            for pick in range(2):
                dot_terms, cross_terms = [], []
                for line in range(LOOK_AZ):
                    left_real = part_ref[earlier, 0, pick, line]
                    left_imag = part_ref[earlier, 1, pick, line]
                    right_real = part_ref[later, 0, pick, line]
                    right_imag = part_ref[later, 1, pick, line]
                    dot_terms += [left_real * right_real, left_imag * right_imag]
                    cross_terms += [left_imag * right_real - left_real * right_imag]
                real.append(total(dot_terms))
                imag.append(total(cross_terms))
            slot = 2 * (owner * pairs_here + index)
            split(split_ref, slot, *real)
            split(split_ref, slot + 1, *imag)
        return carry

    lax.fori_loop(0, owners, one_owner, 0, unroll=2)
    table = window_ref[...]
    date_ref[...] = dot(power_ref[...].reshape(16 * dates, 2 * LANES), table)
    sum_ref[...] = dot(split_ref[...].reshape(32 * pair_total, 2 * LANES), table)
    share = 1.0 / (LOOK_AZ * LOOK_RG)

    def fold(ref, count):
        lane = lax.broadcasted_iota(jnp.int32, (count, LANES), 1)
        look = lane // 16
        source = look % 2 * 8 + look // 4 * 4 + lane // 8 % 2 * 2 + look // 2 % 2
        out = ref[pl.ds(0, count, stride=16), :]
        for pick in range(1, 16):
            out = jnp.where(source == pick, ref[pl.ds(pick, count, stride=16), :], out)
        return out * share

    root_ref[...] = lax.rsqrt(fold(date_ref, dates) + EPSILON)
    for owner in range(owners):
        for index in range(pairs_here):
            earlier = root_ref[pl.ds(pair_ref[owner, index], 1), :]
            later = root_ref[pl.ds(pair_ref[owner, pairs_here + index], 1), :]
            start = 2 * (owner * pairs_here + index)
            scale_ref[start : start + 2, :] = jnp.broadcast_to(earlier * later, (2, LANES))
    ratio = fold(sum_ref, 2 * pair_total) * scale_ref[...]
    out_ref[...] = ratio.reshape(out_ref.shape)


def filter_kernel(
    ratio_ref, sample_high_ref, sample_low_ref, place_table_ref, line_high_ref, line_low_ref,
    back_high_ref, back_low_ref, end_high_ref, end_low_ref,
    filtered_ref, coherence_ref, high_ref, low_ref, size_ref,
):
    pairs = coherence_ref.shape[0]
    lane = lax.broadcasted_iota(jnp.int32, (8, LANES), 1)
    line = lax.broadcasted_iota(jnp.int32, (8, LANES), 0)
    inside = lane // 16 == line
    sources = ratio_ref.shape[0]
    values = ratio_ref[...].reshape(sources * 2 * pairs, LANES)
    square = values * values
    size = jnp.sqrt(square + pltpu.roll(square, square.shape[0] - 1, 0))

    def place(target, start, column, row):
        target[start : start + 8, column * LANES : (column + 1) * LANES] = jnp.where(
            inside, jnp.broadcast_to(row, (8, LANES)), 0.0
        ).astype(target.dtype)

    high = values.astype(jnp.bfloat16).astype(jnp.float32)
    low = values - high
    for source in range(sources):
        core = source & 1
        half = (source >> 1) & 1
        block = core * 4 + (source >> 2)
        for pair in range(pairs):
            start = pair * PATCH + block * 8
            first = (source * pairs + pair) * 2
            for part in range(2):
                pick = slice(first + part, first + part + 1)
                place(high_ref, start, 2 * part + half, high[pick])
                place(low_ref, start, 2 * part + half, low[pick])
            place(size_ref, start, half, size[first : first + 1])
    for pair in range(pairs):
        lines = slice(pair * PATCH, (pair + 1) * PATCH)
        magnitude = dot_rows(place_table_ref[...], size_ref[lines])
        coherence_ref[pair] = magnitude.astype(coherence_ref.dtype)
    spread = (
        dot(high_ref[...], sample_high_ref[...])
        + dot(low_ref[...], sample_high_ref[...])
        + dot(high_ref[...], sample_low_ref[...])
    )
    columns = []
    for half in range(2):
        for pair in range(pairs):
            start = pair * PATCH + half * HALF
            part = spread[start : start + HALF]
            columns.append(jnp.concatenate([part[:, :LANES], part[:, LANES:]], 0))
    high, low = rounded_parts(jnp.concatenate(columns, 1))
    spectrum = (
        dot(line_high_ref[...], high) + dot(line_high_ref[...], low) + dot(line_low_ref[...], high)
    )
    width = pairs * LANES
    top = spectrum[:, :width]
    bottom = spectrum[:, width:]
    sign = 1.0 - 2.0 * (lax.broadcasted_iota(jnp.int32, (PATCH, width), 0) % 2).astype(jnp.float32)
    weighted = []
    for patch in (top, top + sign * bottom, bottom):
        parts = []
        for pair in range(pairs):
            values = patch[:, pair * LANES : (pair + 1) * LANES]
            square = values * values
            energy = square + pltpu.roll(square, LANES // 2, 1)
            weight = lax.rsqrt(lax.rsqrt(energy + 1.0))
            total = jnp.sum(weight, axis=(0, 1), keepdims=True)
            parts.append(values * weight * ((2.0 * PATCH * PATCH) / total))
        weighted.append(jnp.concatenate(parts, 1))
    weighted = [weighted[0], weighted[1], weighted[1], weighted[2]]
    high, low = rounded_parts(jnp.concatenate(weighted, 0))
    back = (
        dot_rows(back_high_ref[...], high)
        + dot_rows(back_high_ref[...], low)
        + dot_rows(back_low_ref[...], high)
    )
    high, low = rounded_parts(jnp.concatenate([back[: width // 2], back[width // 2 :]], 1))
    lines = dot(high, end_high_ref[...]) + dot(low, end_high_ref[...]) + dot(high, end_low_ref[...])
    filtered_ref[...] = lines.reshape(filtered_ref.shape).astype(filtered_ref.dtype)


def fast_local(acquisitions, date_pairs, sizes):
    depth, across, cores = sizes
    total = depth * across * cores
    dates_here, line_count, _, sample_count = acquisitions.shape
    columns = sample_count // LANES
    lines_each = line_count // depth
    rows = lines_each * columns * 2
    look_lines = lines_each // LOOK_AZ
    look_samples = sample_count // LOOK_RG
    cells = look_lines * look_samples
    pairs_here = date_pairs.shape[1]
    pair_total = pairs_here * total
    dates = dates_here * depth
    group = lax.axis_index("date")
    names = ("date", "rng", "az")

    def swap(values, offset):
        return lax.ppermute(values, names, [(i, i ^ offset) for i in range(total)])

    view = acquisitions.reshape(dates_here, line_count, 2, columns, LANES)
    view = view.transpose(0, 1, 3, 2, 4).reshape(dates_here, line_count * columns * 2, LANES)

    def block(source, offset):
        return lax.dynamic_slice_in_dim(source, (group ^ offset) * rows, rows, 1)

    step = across * cores
    received = {offset: swap(block(view, offset), offset * step) for offset in (3, 1, 2)}
    own = block(view, 0)
    listed = jnp.broadcast_to(date_pairs.reshape(1, -1), (total, 2 * pairs_here))
    pair_list = lax.all_to_all(listed, names, 0, 0, tiled=True)
    vmem = pl.BlockSpec(memory_space=pltpu.VMEM)
    smem = pl.BlockSpec(memory_space=pltpu.SMEM)
    ratios = pl.pallas_call(
        products_kernel,
        name="products",
        out_shape=jax.ShapeDtypeStruct((total, 2 * pairs_here, cells), jnp.float32),
        in_specs=[smem, smem] + [vmem] * 5,
        out_specs=vmem,
        scratch_shapes=[
            pltpu.VMEM((dates, 2, 2, LOOK_AZ, 8, LANES), jnp.float32),
            pltpu.VMEM((2 * pair_total, 16, 2 * LANES), jnp.bfloat16),
            pltpu.VMEM((dates, 16, 2 * LANES), jnp.bfloat16),
            pltpu.VMEM((32 * pair_total, cells), jnp.float32),
            pltpu.VMEM((16 * dates, cells), jnp.float32),
            pltpu.VMEM((dates, cells), jnp.float32),
            pltpu.VMEM((2 * pair_total, cells), jnp.float32),
        ],
        compiler_params=pltpu.CompilerParams(vmem_limit_bytes=12 << 20),
    )(
        group.reshape(1),
        pair_list,
        own,
        received[1],
        received[2],
        received[3],
        jnp.asarray(window_table(cells)),
    )
    arrived = lax.all_to_all(ratios, names, 0, 0, tiled=True)
    sample_table, place_table = sample_tables(cells, look_samples, across)
    line_table, end_table = line_tables()
    tables = []
    for table in (sample_table, None, line_table, back_table(pairs_here), end_table):
        tables += [place_table] if table is None else list(split_table(table))
    filtered, coherence = pl.pallas_call(
        filter_kernel,
        name="filter",
        out_shape=[
            jax.ShapeDtypeStruct((pairs_here, 2, HALF, PATCH), jnp.bfloat16),
            jax.ShapeDtypeStruct((pairs_here, HALF, PATCH), jnp.bfloat16),
        ],
        in_specs=[vmem] * (1 + len(tables)),
        out_specs=[vmem, vmem],
        scratch_shapes=[
            pltpu.VMEM((pairs_here * PATCH, 2 * across * cells), jnp.bfloat16),
            pltpu.VMEM((pairs_here * PATCH, 2 * across * cells), jnp.bfloat16),
            pltpu.VMEM((pairs_here * PATCH, across * cells), jnp.bfloat16),
        ],
        compiler_params=pltpu.CompilerParams(vmem_limit_bytes=8 << 20),
    )(arrived, *[jnp.asarray(t) for t in tables])
    return (filtered.transpose(0, 1, 3, 2), coherence.transpose(0, 2, 1))


def fits(acquisitions, date_pairs, sizes):
    depth, across, cores = sizes
    _, line_count, _, sample_count = acquisitions.shape
    look_lines = line_count // depth // LOOK_AZ
    look_samples = sample_count // LOOK_RG
    return (
        sizes == (4, 2, 2)
        and line_count % (depth * LOOK_AZ) == 0
        and sample_count == 2 * LANES
        and look_lines == 8
        and look_lines * look_samples == LANES
        and line_count * cores == LOOK_AZ * PATCH
        and sample_count * across == LOOK_RG * HALF
        and date_pairs.shape[1] == 2
    )


def solution(mesh):
    sizes = tuple(mesh.shape[name] for name in ("date", "rng", "az"))

    def chosen(acquisitions, date_pairs):
        if fits(acquisitions, date_pairs, sizes):
            return fast_local(acquisitions, date_pairs, sizes)
        return local(acquisitions, date_pairs)

    return jax.shard_map(
        chosen,
        mesh=mesh,
        in_specs=(P(("tile", "date"), "az", None, "rng"), P(None, ("date", "rng", "az"))),
        out_specs=(
            P(("tile", "date", "rng", "az"), None, None, None),
            P(("tile", "date", "rng", "az"), None, None),
        ),
        check_vma=False,
    )
```

```python
import math

import jax
import jax.numpy as jnp
import numpy as np
from jax import lax
from jax.experimental import pallas as pl
from jax.experimental.pallas import tpu as pltpu
from jax.sharding import PartitionSpec as P


PATCH = 64
LOOK_AZ = 4
LOOK_RG = 16
HALF = 32
LANES = 128


EPSILON = 1e-06
HIGHEST = lax.Precision.HIGHEST


def fourier_tables(length):
    position = jnp.arange(length, dtype=jnp.int32)
    product = position[:, None] * position[None, :] % length
    angle = product.astype(jnp.float32) * (2.0 * math.pi / length)
    return (jnp.cos(angle), jnp.sin(angle))


def taper_window(length):
    midway = length // 2
    position = jnp.arange(length, dtype=jnp.float32)
    ramp_line = 1.0 - jnp.abs(position + 0.5 - midway) / midway
    return ramp_line[:, None] * ramp_line[None, :]


def transform(real_part, imag_part, cosine_table, sine_table, inverse):
    length = cosine_table.shape[0]
    if inverse:
        matrix = jnp.concatenate(
            [
                jnp.concatenate([cosine_table, sine_table], 1),
                jnp.concatenate([-sine_table, cosine_table], 1),
            ],
            0,
        )
    else:
        matrix = jnp.concatenate(
            [
                jnp.concatenate([cosine_table, -sine_table], 1),
                jnp.concatenate([sine_table, cosine_table], 1),
            ],
            0,
        )
    joined = jnp.concatenate([real_part, imag_part], axis=-1)
    across = jnp.einsum("bnc,cd->bnd", joined, matrix, precision=HIGHEST)
    rotated = jnp.einsum(
        "tkn,bnd->btkd", jnp.stack([cosine_table, sine_table]), across, precision=HIGHEST
    )
    with_cosine = rotated[:, 0]
    with_sine = rotated[:, 1]
    if inverse:
        scaling = 1.0 / (length * length)
        out_real = (with_cosine[..., :length] - with_sine[..., length:]) * scaling
        out_imag = (with_cosine[..., length:] + with_sine[..., :length]) * scaling
    else:
        out_real = with_cosine[..., :length] + with_sine[..., length:]
        out_imag = with_cosine[..., length:] - with_sine[..., :length]
    return (out_real, out_imag)


def goldstein(
    extended_real, extended_imag, cosine_table, sine_table, window, block_lines, block_samples
):
    groups = extended_real.shape[0]
    extent_line = extended_real.shape[1]
    extent_sample = extended_real.shape[2]
    length = cosine_table.shape[0]
    midway = length // 2
    summed_real = jnp.zeros_like(extended_real)
    summed_imag = jnp.zeros_like(extended_imag)
    for start_line in (0, midway):
        for start_sample in (0, midway):
            count_line = (extent_line - start_line) // length
            count_sample = (extent_sample - start_sample) // length
            stop_line = start_line + count_line * length
            stop_sample = start_sample + count_sample * length

            def extract(values):
                region = values[:, start_line:stop_line, start_sample:stop_sample]
                region = region.reshape(groups, count_line, length, count_sample, length)
                return region.transpose(0, 1, 3, 2, 4).reshape(-1, length, length)

            def insert(values):
                shaped = (values * window).reshape(groups, count_line, count_sample, length, length)
                return shaped.transpose(0, 1, 3, 2, 4).reshape(
                    groups, count_line * length, count_sample * length
                )

            spec_real, spec_imag = transform(
                extract(extended_real), extract(extended_imag), cosine_table, sine_table, False
            )
            energy = spec_real * spec_real + spec_imag * spec_imag
            weight = (energy + 1.0) ** 0.25
            weight = weight / jnp.mean(weight, axis=(1, 2), keepdims=True)
            back_real, back_imag = transform(
                spec_real * weight, spec_imag * weight, cosine_table, sine_table, True
            )
            summed_real = summed_real.at[:, start_line:stop_line, start_sample:stop_sample].add(
                insert(back_real)
            )
            summed_imag = summed_imag.at[:, start_line:stop_line, start_sample:stop_sample].add(
                insert(back_imag)
            )
    center_real = summed_real[:, midway : midway + block_lines, midway : midway + block_samples]
    center_imag = summed_imag[:, midway : midway + block_lines, midway : midway + block_samples]
    return (center_real, center_imag)


def local(acquisitions, date_pairs):
    every_pair = lax.all_gather(date_pairs, ("date", "rng", "az"), axis=1, tiled=True)
    by_lines = lax.all_to_all(acquisitions, "date", split_axis=1, concat_axis=0, tiled=True)
    line_count = by_lines.shape[1]
    sample_count = by_lines.shape[3]
    look_lines = line_count // LOOK_AZ
    look_samples = sample_count // LOOK_RG

    def take_looks(values):
        leading = values.shape[:-2]
        shaped = values.reshape(leading + (look_lines, LOOK_AZ, look_samples, LOOK_RG))
        return jnp.sum(shaped, axis=(-3, -1)) * (1.0 / (LOOK_AZ * LOOK_RG))

    real_lines = by_lines[:, :, 0, :].astype(jnp.float32)
    imag_lines = by_lines[:, :, 1, :].astype(jnp.float32)
    intensity = take_looks(real_lines * real_lines + imag_lines * imag_lines)
    pair_total = every_pair.shape[1]
    block_rows = math.gcd(pair_total, 32)
    turns = pair_total // block_rows
    earlier = every_pair[0].reshape(turns, block_rows)
    later = every_pair[1].reshape(turns, block_rows)

    def cross_block(indices):
        left = jnp.take(by_lines, indices[0], axis=0).astype(jnp.float32)
        right = jnp.take(by_lines, indices[1], axis=0).astype(jnp.float32)
        cross_real = take_looks(left[:, :, 0] * right[:, :, 0] + left[:, :, 1] * right[:, :, 1])
        cross_imag = take_looks(left[:, :, 1] * right[:, :, 0] - left[:, :, 0] * right[:, :, 1])
        return (cross_real, cross_imag)

    cross_real, cross_imag = lax.map(cross_block, (earlier, later))
    cross_real = cross_real.reshape(pair_total, look_lines, look_samples)
    cross_imag = cross_imag.reshape(pair_total, look_lines, look_samples)
    power_early = jnp.take(intensity, every_pair[0], axis=0)
    power_late = jnp.take(intensity, every_pair[1], axis=0)
    denominator = jnp.sqrt((power_early + EPSILON) * (power_late + EPSILON))
    payload = jnp.stack([cross_real / denominator, cross_imag / denominator], axis=1)
    partway = lax.all_to_all(
        lax.all_to_all(payload, "date", split_axis=0, concat_axis=2, tiled=True),
        "rng",
        split_axis=0,
        concat_axis=3,
        tiled=True,
    )
    returned = lax.all_to_all(partway, "az", split_axis=0, concat_axis=2, tiled=True)
    ratio_real = returned[:, 0]
    ratio_imag = returned[:, 1]
    coherence = jnp.sqrt(ratio_real * ratio_real + ratio_imag * ratio_imag).astype(jnp.bfloat16)
    block_lines = ratio_real.shape[1]
    block_samples = ratio_real.shape[2]
    padding = ((0, 0), (HALF, HALF), (HALF, HALF))
    extended_real = jnp.pad(ratio_real, padding)
    extended_imag = jnp.pad(ratio_imag, padding)
    cosine_table, sine_table = fourier_tables(PATCH)
    window = taper_window(PATCH)
    out_real, out_imag = goldstein(
        extended_real, extended_imag, cosine_table, sine_table, window, block_lines, block_samples
    )
    filtered = jnp.stack([out_real, out_imag], axis=1).astype(jnp.bfloat16)
    return (filtered, coherence)


def rounded_parts(values):
    high = values.astype(jnp.bfloat16)
    low = (values - high.astype(jnp.float32)).astype(jnp.bfloat16)
    return (high, low)


def split_table(table, axis):
    table = np.asarray(table, np.float32)
    high = table.astype(jnp.bfloat16)
    low = (table - high.astype(np.float32)).astype(jnp.bfloat16)
    return np.concatenate([high, high, low], axis)


def three_parts(values, axis):
    high, low = rounded_parts(values)
    return jnp.concatenate([high, low, high], axis)


def window_table(cells):
    lane = np.arange(LANES)
    table = lane[:, None] // LOOK_RG == np.arange(cells)[None, :] % (LANES // LOOK_RG)
    return np.concatenate([table, table], 0).astype(np.float32).astype(jnp.bfloat16)


def sample_tables(cells, samples, halves):
    cell = np.arange(cells) % samples
    frequency = np.arange(PATCH)
    forward = []
    place = []
    for half in range(halves):
        position = half * samples + cell
        angle = 2.0 * np.pi * (position[:, None] * frequency[None, :] % PATCH) / PATCH
        forward.append((np.cos(angle), np.sin(angle)))
        place.append(np.arange(halves * samples)[:, None] == position[None, :])
    real = [np.concatenate([c, -s], 1) for c, s in forward]
    imag = [np.concatenate([s, c], 1) for c, s in forward]
    return (
        np.concatenate(real + imag, 0),
        np.concatenate(place, 1).astype(np.float32).astype(jnp.bfloat16),
    )


def line_tables():
    row = np.arange(HALF)
    frequency = np.arange(PATCH)
    angle = 2.0 * np.pi * (frequency[:, None] * row[None, :] % PATCH) / PATCH
    cosine, sine = np.cos(angle), np.sin(angle)
    ramp = 1.0 - np.abs(np.arange(PATCH) + 0.5 - HALF) / HALF
    first, second = ramp[None, :HALF], ramp[None, HALF:]
    flip = (1.0 - 2.0 * (frequency % 2))[:, None]
    none = np.zeros_like(angle)

    def back(wave):
        top = np.concatenate([second * wave, first * wave, none, none], 0)
        bottom = np.concatenate([none, none, second * flip * wave, first * wave], 0)
        return np.concatenate([top, bottom], 1)

    end = np.concatenate([back(cosine), back(sine)], 0) / PATCH**2
    return (np.concatenate([cosine, sine], 1), end)


def back_table(pairs):
    frequency = np.arange(PATCH)
    column = np.arange(HALF)
    angle = 2.0 * np.pi * (column[:, None] * frequency[None, :] % PATCH) / PATCH
    c, s = np.cos(angle), np.sin(angle)
    direct = np.concatenate([np.concatenate([c, -s], 1), np.concatenate([s, c], 1)], 0)
    turned = np.concatenate([np.concatenate([-s, -c], 1), np.concatenate([c, -s], 1)], 0)
    identity = np.eye(pairs)
    table = np.concatenate([np.kron(identity, direct), np.kron(identity, turned)], 0)
    table = table.reshape(-1, pairs, 2, PATCH).transpose(0, 2, 1, 3)
    return table.reshape(-1, 2 * pairs * PATCH)


def dot(left, right):
    return jnp.dot(left, right, preferred_element_type=jnp.float32)


def dot_rows(left, right):
    return lax.dot_general(
        left, right, (((1,), (1,)), ((), ())), preferred_element_type=jnp.float32
    )


def products_kernel(
    place_ref, pair_ref, own_ref, near_ref, far_ref, last_ref, window_ref,
    out_ref,
    part_ref, split_ref, power_ref, sum_ref, date_ref, root_ref, scale_ref,
):
    group = place_ref[0]
    dates_here = own_ref.shape[0]
    dates = part_ref.shape[0]
    owners = pair_ref.shape[0]
    pairs_here = pair_ref.shape[1] // 2
    pair_total = owners * pairs_here
    row = lax.broadcasted_iota(jnp.int32, (8, LANES), 0)
    low = row < 4
    even = row % 2 == 0

    def split(target, slot, first, second):
        high, rest = rounded_parts(jnp.concatenate([first, second], axis=0))
        target[slot, :, :LANES] = high
        target[slot, :, LANES:] = rest

    def total(terms):
        while len(terms) > 1:
            terms = [a + b for a, b in zip(terms[::2], terms[1::2])]
        return terms[0]

    for offset, ref in enumerate((own_ref, near_ref, far_ref, last_ref)):
        base = (group ^ offset) * dates_here
        for index in range(dates_here):
            values = ref[index].astype(jnp.float32).reshape(8, 2, 8, LANES)
            for pick in range(2):
                squares = []
                for part in range(2):
                    lines = []
                    for look in (pick, pick + 2):
                        upper, lower = values[look, part], values[look + 4, part]
                        lines.append(
                            (
                                jnp.where(low, upper, pltpu.roll(lower, 4, 0)),
                                jnp.where(low, pltpu.roll(upper, 4, 0), lower),
                            )
                        )
                    for line in range(2):
                        first, second = lines[0][line], lines[1][line]
                        real = jnp.where(even, first, pltpu.roll(second, 1, 0))
                        imag = jnp.where(even, pltpu.roll(first, 7, 0), second)
                        part_ref[base + index, 0, pick, 2 * part + line] = real
                        part_ref[base + index, 1, pick, 2 * part + line] = imag
                        squares += [real * real, imag * imag]
                high, rest = rounded_parts(total(squares))
                power_ref[base + index, 8 * pick : 8 * pick + 8, :LANES] = high
                power_ref[base + index, 8 * pick : 8 * pick + 8, LANES:] = rest

    def one_owner(owner, carry):
        for index in range(pairs_here):
            earlier = pair_ref[owner, index]
            later = pair_ref[owner, pairs_here + index]
            real, imag = [], []
            for pick in range(2):
                dot_terms, cross_terms = [], []
                for line in range(LOOK_AZ):
                    left_real = part_ref[earlier, 0, pick, line]
                    left_imag = part_ref[earlier, 1, pick, line]
                    right_real = part_ref[later, 0, pick, line]
                    right_imag = part_ref[later, 1, pick, line]
                    dot_terms += [left_real * right_real, left_imag * right_imag]
                    cross_terms += [left_imag * right_real - left_real * right_imag]
                real.append(total(dot_terms))
                imag.append(total(cross_terms))
            slot = 2 * (owner * pairs_here + index)
            split(split_ref, slot, *real)
            split(split_ref, slot + 1, *imag)
        return carry

    lax.fori_loop(0, owners, one_owner, 0, unroll=owners)
    table = window_ref[...]
    date_ref[...] = dot(power_ref[...].reshape(16 * dates, 2 * LANES), table)
    sum_ref[...] = dot(split_ref[...].reshape(32 * pair_total, 2 * LANES), table)
    share = 1.0 / (LOOK_AZ * LOOK_RG)

    def fold(ref, count):
        lane = lax.broadcasted_iota(jnp.int32, (count, LANES), 1)
        look = lane // 16
        source = look % 2 * 8 + look // 4 * 4 + lane // 8 % 2 * 2 + look // 2 % 2
        out = ref[pl.ds(0, count, stride=16), :]
        for pick in range(1, 16):
            out = jnp.where(source == pick, ref[pl.ds(pick, count, stride=16), :], out)
        return out * share

    root_ref[...] = lax.rsqrt(fold(date_ref, dates) + EPSILON)
    for owner in range(owners):
        for index in range(pairs_here):
            earlier = root_ref[pl.ds(pair_ref[owner, index], 1), :]
            later = root_ref[pl.ds(pair_ref[owner, pairs_here + index], 1), :]
            start = 2 * (owner * pairs_here + index)
            scale_ref[start : start + 2, :] = jnp.broadcast_to(earlier * later, (2, LANES))
    ratio = fold(sum_ref, 2 * pair_total) * scale_ref[...]
    out_ref[...] = ratio.reshape(out_ref.shape)


def filter_kernel(
    ratio_ref, sample_ref, place_table_ref, line_ref, back_ref, end_ref,
    filtered_ref, coherence_ref, high_ref, low_ref, size_ref,
):
    pairs = coherence_ref.shape[0]
    lane = lax.broadcasted_iota(jnp.int32, (8, LANES), 1)
    line = lax.broadcasted_iota(jnp.int32, (8, LANES), 0)
    inside = lane // 16 == line
    sources = ratio_ref.shape[0]
    values = ratio_ref[...].reshape(sources * 2 * pairs, LANES)
    square = values * values
    size = jnp.sqrt(square + pltpu.roll(square, square.shape[0] - 1, 0))

    def place(target, start, column, row):
        target[start : start + 8, column * LANES : (column + 1) * LANES] = jnp.where(
            inside, jnp.broadcast_to(row, (8, LANES)), 0.0
        ).astype(target.dtype)

    high = values.astype(jnp.bfloat16).astype(jnp.float32)
    low = values - high
    for source in range(sources):
        core = source & 1
        half = (source >> 1) & 1
        block = core * 4 + (source >> 2)
        for pair in range(pairs):
            start = pair * PATCH + block * 8
            first = (source * pairs + pair) * 2
            for part in range(2):
                pick = slice(first + part, first + part + 1)
                place(high_ref, start, 2 * part + half, high[pick])
                place(low_ref, start, 2 * part + half, low[pick])
            place(size_ref, start, half, size[first : first + 1])
    for pair in range(pairs):
        lines = slice(pair * PATCH, (pair + 1) * PATCH)
        magnitude = dot_rows(place_table_ref[...], size_ref[lines])
        coherence_ref[pair] = magnitude.astype(coherence_ref.dtype)
    spread = dot(
        jnp.concatenate([high_ref[...], low_ref[...], high_ref[...]], 1), sample_ref[...]
    )
    left = lax.broadcasted_iota(jnp.int32, (HALF, LANES), 1) < PATCH
    columns = []
    for half in range(2):
        first = spread[half * HALF : (half + 1) * HALF]
        second = spread[PATCH + half * HALF : PATCH + (half + 1) * HALF]
        real = jnp.where(left, first, pltpu.roll(second, PATCH, 1))
        imag = jnp.where(left, pltpu.roll(first, PATCH, 1), second)
        columns.append(jnp.concatenate([real, imag], 0))
        columns.append(jnp.concatenate([imag, -real], 0))
    spectrum = dot(line_ref[...], three_parts(jnp.concatenate(columns, 1), 0))
    top_real, top_imag, low_real, low_imag = (
        spectrum[:, index * LANES : (index + 1) * LANES] for index in range(4)
    )
    sign = 1.0 - 2.0 * (lax.broadcasted_iota(jnp.int32, (PATCH, LANES), 0) % 2).astype(jnp.float32)
    side = lax.broadcasted_iota(jnp.int32, (1, LANES), 1) < PATCH
    weighted = []
    for real, imag in (
        (top_real, top_imag),
        (top_real + sign * low_real, top_imag + sign * low_imag),
        (low_real, low_imag),
    ):
        weight = lax.rsqrt(lax.rsqrt(real * real + imag * imag + 1.0))
        total = jnp.sum(weight, axis=0, keepdims=True)
        first = jnp.sum(jnp.where(side, total, 0.0), axis=1, keepdims=True)
        second = jnp.sum(jnp.where(side, 0.0, total), axis=1, keepdims=True)
        weight = weight * ((1.0 * PATCH * PATCH) / jnp.where(side, first, second))
        weighted.append(three_parts(jnp.concatenate([real * weight, imag * weight], 1), 1))
    back = dot_rows(
        back_ref[...],
        jnp.concatenate([weighted[0], weighted[1], weighted[1], weighted[2]], 0),
    )
    count = back.shape[0] // 2
    lines = dot(
        three_parts(jnp.concatenate([back[:count], back[count:]], 1), 1), end_ref[...]
    )
    filtered_ref[...] = lines.reshape(filtered_ref.shape).astype(filtered_ref.dtype)


def fast_local(acquisitions, date_pairs, sizes):
    depth, across, cores = sizes
    total = depth * across * cores
    dates_here, line_count, _, sample_count = acquisitions.shape
    columns = sample_count // LANES
    lines_each = line_count // depth
    rows = lines_each * columns * 2
    look_lines = lines_each // LOOK_AZ
    look_samples = sample_count // LOOK_RG
    cells = look_lines * look_samples
    pairs_here = date_pairs.shape[1]
    pair_total = pairs_here * total
    dates = dates_here * depth
    group = lax.axis_index("date")
    names = ("date", "rng", "az")

    def swap(values, offset):
        return lax.ppermute(values, names, [(i, i ^ offset) for i in range(total)])

    view = acquisitions.reshape(dates_here, line_count, 2, columns, LANES)
    view = view.transpose(0, 1, 3, 2, 4).reshape(dates_here, line_count * columns * 2, LANES)

    step = across * cores
    vmem = pl.BlockSpec(memory_space=pltpu.VMEM)
    smem = pl.BlockSpec(memory_space=pltpu.SMEM)

    def block(offset):
        return lax.dynamic_slice_in_dim(view, (group ^ offset) * rows, rows, 1)

    received = {offset: swap(block(offset), offset * step) for offset in (3, 1, 2)}
    own = block(0)
    listed = jnp.broadcast_to(date_pairs.reshape(1, -1), (total, 2 * pairs_here))
    pair_list = lax.all_to_all(listed, names, 0, 0, tiled=True)
    ratios = pl.pallas_call(
        products_kernel,
        name="products",
        out_shape=jax.ShapeDtypeStruct((total, 2 * pairs_here, cells), jnp.float32),
        in_specs=[smem, smem] + [vmem] * 5,
        out_specs=vmem,
        scratch_shapes=[
            pltpu.VMEM((dates, 2, 2, LOOK_AZ, 8, LANES), jnp.float32),
            pltpu.VMEM((2 * pair_total, 16, 2 * LANES), jnp.bfloat16),
            pltpu.VMEM((dates, 16, 2 * LANES), jnp.bfloat16),
            pltpu.VMEM((32 * pair_total, cells), jnp.float32),
            pltpu.VMEM((16 * dates, cells), jnp.float32),
            pltpu.VMEM((dates, cells), jnp.float32),
            pltpu.VMEM((2 * pair_total, cells), jnp.float32),
        ],
        compiler_params=pltpu.CompilerParams(vmem_limit_bytes=12 << 20),
    )(
        group.reshape(1),
        pair_list,
        own,
        received[1],
        received[2],
        received[3],
        jnp.asarray(window_table(cells)),
    )
    arrived = lax.all_to_all(ratios, names, 0, 0, tiled=True)
    sample_table, place_table = sample_tables(cells, look_samples, across)
    line_table, end_table = line_tables()
    tables = [
        split_table(sample_table, 0),
        place_table,
        split_table(line_table, 1),
        split_table(back_table(pairs_here), 1),
        split_table(end_table, 0),
    ]
    filtered, coherence = pl.pallas_call(
        filter_kernel,
        name="filter",
        out_shape=[
            jax.ShapeDtypeStruct((pairs_here, 2, HALF, PATCH), jnp.bfloat16),
            jax.ShapeDtypeStruct((pairs_here, HALF, PATCH), jnp.bfloat16),
        ],
        in_specs=[vmem] * (1 + len(tables)),
        out_specs=[vmem, vmem],
        scratch_shapes=[
            pltpu.VMEM((pairs_here * PATCH, 2 * across * cells), jnp.bfloat16),
            pltpu.VMEM((pairs_here * PATCH, 2 * across * cells), jnp.bfloat16),
            pltpu.VMEM((pairs_here * PATCH, across * cells), jnp.bfloat16),
        ],
        compiler_params=pltpu.CompilerParams(vmem_limit_bytes=8 << 20),
    )(arrived, *[jnp.asarray(t) for t in tables])
    return (filtered.transpose(0, 1, 3, 2), coherence.transpose(0, 2, 1))


def fits(acquisitions, date_pairs, sizes):
    depth, across, cores = sizes
    _, line_count, _, sample_count = acquisitions.shape
    look_lines = line_count // depth // LOOK_AZ
    look_samples = sample_count // LOOK_RG
    return (
        sizes == (4, 2, 2)
        and line_count % (depth * LOOK_AZ) == 0
        and sample_count == 2 * LANES
        and look_lines == 8
        and look_lines * look_samples == LANES
        and line_count * cores == LOOK_AZ * PATCH
        and sample_count * across == LOOK_RG * HALF
        and date_pairs.shape[1] == 2
    )


def solution(mesh):
    sizes = tuple(mesh.shape[name] for name in ("date", "rng", "az"))

    def chosen(acquisitions, date_pairs):
        if fits(acquisitions, date_pairs, sizes):
            return fast_local(acquisitions, date_pairs, sizes)
        return local(acquisitions, date_pairs)

    return jax.shard_map(
        chosen,
        mesh=mesh,
        in_specs=(P(("tile", "date"), "az", None, "rng"), P(None, ("date", "rng", "az"))),
        out_specs=(
            P(("tile", "date", "rng", "az"), None, None, None),
            P(("tile", "date", "rng", "az"), None, None),
        ),
        check_vma=False,
    )
```

```python
import math

import jax
import jax.numpy as jnp
import numpy as np
from jax import lax
from jax.experimental import pallas as pl
from jax.experimental.pallas import tpu as pltpu
from jax.sharding import PartitionSpec as P


PATCH = 64
LOOK_AZ = 4
LOOK_RG = 16
HALF = 32
LANES = 128


EPSILON = 1e-06
HIGHEST = lax.Precision.HIGHEST


def fourier_tables(length):
    position = jnp.arange(length, dtype=jnp.int32)
    product = position[:, None] * position[None, :] % length
    angle = product.astype(jnp.float32) * (2.0 * math.pi / length)
    return (jnp.cos(angle), jnp.sin(angle))


def taper_window(length):
    midway = length // 2
    position = jnp.arange(length, dtype=jnp.float32)
    ramp_line = 1.0 - jnp.abs(position + 0.5 - midway) / midway
    return ramp_line[:, None] * ramp_line[None, :]


def transform(real_part, imag_part, cosine_table, sine_table, inverse):
    length = cosine_table.shape[0]
    if inverse:
        matrix = jnp.concatenate(
            [
                jnp.concatenate([cosine_table, sine_table], 1),
                jnp.concatenate([-sine_table, cosine_table], 1),
            ],
            0,
        )
    else:
        matrix = jnp.concatenate(
            [
                jnp.concatenate([cosine_table, -sine_table], 1),
                jnp.concatenate([sine_table, cosine_table], 1),
            ],
            0,
        )
    joined = jnp.concatenate([real_part, imag_part], axis=-1)
    across = jnp.einsum("bnc,cd->bnd", joined, matrix, precision=HIGHEST)
    rotated = jnp.einsum(
        "tkn,bnd->btkd", jnp.stack([cosine_table, sine_table]), across, precision=HIGHEST
    )
    with_cosine = rotated[:, 0]
    with_sine = rotated[:, 1]
    if inverse:
        scaling = 1.0 / (length * length)
        out_real = (with_cosine[..., :length] - with_sine[..., length:]) * scaling
        out_imag = (with_cosine[..., length:] + with_sine[..., :length]) * scaling
    else:
        out_real = with_cosine[..., :length] + with_sine[..., length:]
        out_imag = with_cosine[..., length:] - with_sine[..., :length]
    return (out_real, out_imag)


def goldstein(
    extended_real, extended_imag, cosine_table, sine_table, window, block_lines, block_samples
):
    groups = extended_real.shape[0]
    extent_line = extended_real.shape[1]
    extent_sample = extended_real.shape[2]
    length = cosine_table.shape[0]
    midway = length // 2
    summed_real = jnp.zeros_like(extended_real)
    summed_imag = jnp.zeros_like(extended_imag)
    for start_line in (0, midway):
        for start_sample in (0, midway):
            count_line = (extent_line - start_line) // length
            count_sample = (extent_sample - start_sample) // length
            stop_line = start_line + count_line * length
            stop_sample = start_sample + count_sample * length

            def extract(values):
                region = values[:, start_line:stop_line, start_sample:stop_sample]
                region = region.reshape(groups, count_line, length, count_sample, length)
                return region.transpose(0, 1, 3, 2, 4).reshape(-1, length, length)

            def insert(values):
                shaped = (values * window).reshape(groups, count_line, count_sample, length, length)
                return shaped.transpose(0, 1, 3, 2, 4).reshape(
                    groups, count_line * length, count_sample * length
                )

            spec_real, spec_imag = transform(
                extract(extended_real), extract(extended_imag), cosine_table, sine_table, False
            )
            energy = spec_real * spec_real + spec_imag * spec_imag
            weight = (energy + 1.0) ** 0.25
            weight = weight / jnp.mean(weight, axis=(1, 2), keepdims=True)
            back_real, back_imag = transform(
                spec_real * weight, spec_imag * weight, cosine_table, sine_table, True
            )
            summed_real = summed_real.at[:, start_line:stop_line, start_sample:stop_sample].add(
                insert(back_real)
            )
            summed_imag = summed_imag.at[:, start_line:stop_line, start_sample:stop_sample].add(
                insert(back_imag)
            )
    center_real = summed_real[:, midway : midway + block_lines, midway : midway + block_samples]
    center_imag = summed_imag[:, midway : midway + block_lines, midway : midway + block_samples]
    return (center_real, center_imag)


def local(acquisitions, date_pairs):
    every_pair = lax.all_gather(date_pairs, ("date", "rng", "az"), axis=1, tiled=True)
    by_lines = lax.all_to_all(acquisitions, "date", split_axis=1, concat_axis=0, tiled=True)
    line_count = by_lines.shape[1]
    sample_count = by_lines.shape[3]
    look_lines = line_count // LOOK_AZ
    look_samples = sample_count // LOOK_RG

    def take_looks(values):
        leading = values.shape[:-2]
        shaped = values.reshape(leading + (look_lines, LOOK_AZ, look_samples, LOOK_RG))
        return jnp.sum(shaped, axis=(-3, -1)) * (1.0 / (LOOK_AZ * LOOK_RG))

    real_lines = by_lines[:, :, 0, :].astype(jnp.float32)
    imag_lines = by_lines[:, :, 1, :].astype(jnp.float32)
    intensity = take_looks(real_lines * real_lines + imag_lines * imag_lines)
    pair_total = every_pair.shape[1]
    block_rows = math.gcd(pair_total, 32)
    turns = pair_total // block_rows
    earlier = every_pair[0].reshape(turns, block_rows)
    later = every_pair[1].reshape(turns, block_rows)

    def cross_block(indices):
        left = jnp.take(by_lines, indices[0], axis=0).astype(jnp.float32)
        right = jnp.take(by_lines, indices[1], axis=0).astype(jnp.float32)
        cross_real = take_looks(left[:, :, 0] * right[:, :, 0] + left[:, :, 1] * right[:, :, 1])
        cross_imag = take_looks(left[:, :, 1] * right[:, :, 0] - left[:, :, 0] * right[:, :, 1])
        return (cross_real, cross_imag)

    cross_real, cross_imag = lax.map(cross_block, (earlier, later))
    cross_real = cross_real.reshape(pair_total, look_lines, look_samples)
    cross_imag = cross_imag.reshape(pair_total, look_lines, look_samples)
    power_early = jnp.take(intensity, every_pair[0], axis=0)
    power_late = jnp.take(intensity, every_pair[1], axis=0)
    denominator = jnp.sqrt((power_early + EPSILON) * (power_late + EPSILON))
    payload = jnp.stack([cross_real / denominator, cross_imag / denominator], axis=1)
    partway = lax.all_to_all(
        lax.all_to_all(payload, "date", split_axis=0, concat_axis=2, tiled=True),
        "rng",
        split_axis=0,
        concat_axis=3,
        tiled=True,
    )
    returned = lax.all_to_all(partway, "az", split_axis=0, concat_axis=2, tiled=True)
    ratio_real = returned[:, 0]
    ratio_imag = returned[:, 1]
    coherence = jnp.sqrt(ratio_real * ratio_real + ratio_imag * ratio_imag).astype(jnp.bfloat16)
    block_lines = ratio_real.shape[1]
    block_samples = ratio_real.shape[2]
    padding = ((0, 0), (HALF, HALF), (HALF, HALF))
    extended_real = jnp.pad(ratio_real, padding)
    extended_imag = jnp.pad(ratio_imag, padding)
    cosine_table, sine_table = fourier_tables(PATCH)
    window = taper_window(PATCH)
    out_real, out_imag = goldstein(
        extended_real, extended_imag, cosine_table, sine_table, window, block_lines, block_samples
    )
    filtered = jnp.stack([out_real, out_imag], axis=1).astype(jnp.bfloat16)
    return (filtered, coherence)


def rounded_parts(values):
    high = values.astype(jnp.bfloat16)
    low = (values - high.astype(jnp.float32)).astype(jnp.bfloat16)
    return (high, low)


def split_table(table, axis):
    table = np.asarray(table, np.float32)
    high = table.astype(jnp.bfloat16)
    low = (table - high.astype(np.float32)).astype(jnp.bfloat16)
    return np.concatenate([high, high, low], axis)


def three_parts(values, axis):
    high, low = rounded_parts(values)
    return jnp.concatenate([high, low, high], axis)


def window_table(cells):
    lane = np.arange(LANES)
    table = lane[:, None] // LOOK_RG == np.arange(cells)[None, :] % (LANES // LOOK_RG)
    return np.concatenate([table, table], 0).astype(np.float32).astype(jnp.bfloat16)


def sample_tables(cells, samples, halves):
    cell = np.arange(cells) % samples
    frequency = np.arange(PATCH)
    forward = []
    place = []
    for half in range(halves):
        position = half * samples + cell
        angle = 2.0 * np.pi * (position[:, None] * frequency[None, :] % PATCH) / PATCH
        forward.append((np.cos(angle), np.sin(angle)))
        place.append(np.arange(halves * samples)[:, None] == position[None, :])
    real = [np.concatenate([c, -s], 1) for c, s in forward]
    imag = [np.concatenate([s, c], 1) for c, s in forward]
    return (
        np.concatenate(real + imag, 0),
        np.concatenate(place, 1).astype(np.float32).astype(jnp.bfloat16),
    )


def line_tables():
    row = np.arange(HALF)
    frequency = np.arange(PATCH)
    angle = 2.0 * np.pi * (frequency[:, None] * row[None, :] % PATCH) / PATCH
    cosine, sine = np.cos(angle), np.sin(angle)
    ramp = 1.0 - np.abs(np.arange(PATCH) + 0.5 - HALF) / HALF
    first, second = ramp[None, :HALF], ramp[None, HALF:]
    flip = (1.0 - 2.0 * (frequency % 2))[:, None]
    none = np.zeros_like(angle)

    def back(wave):
        top = np.concatenate([second * wave, first * wave, none, none], 0)
        bottom = np.concatenate([none, none, second * flip * wave, first * wave], 0)
        return np.concatenate([top, bottom], 1)

    end = np.concatenate([back(cosine), back(sine)], 0) / PATCH**2
    end = np.concatenate([end, np.zeros((end.shape[0], 2 * LANES - PATCH))], 1)
    return (np.concatenate([cosine, sine], 1), end)


def back_table(pairs):
    frequency = np.arange(PATCH)
    column = np.arange(HALF)
    angle = 2.0 * np.pi * (column[:, None] * frequency[None, :] % PATCH) / PATCH
    c, s = np.cos(angle), np.sin(angle)
    direct = np.concatenate([np.concatenate([c, -s], 1), np.concatenate([s, c], 1)], 0)
    turned = np.concatenate([np.concatenate([-s, -c], 1), np.concatenate([c, -s], 1)], 0)
    identity = np.eye(pairs)
    table = np.concatenate([np.kron(identity, direct), np.kron(identity, turned)], 0)
    table = table.reshape(-1, pairs, 2, PATCH).transpose(0, 2, 1, 3)
    return table.reshape(-1, 2 * pairs * PATCH)


def dot(left, right):
    return jnp.dot(left, right, preferred_element_type=jnp.float32)


def dot_rows(left, right):
    return lax.dot_general(
        left, right, (((1,), (1,)), ((), ())), preferred_element_type=jnp.float32
    )


def total(terms):
    while len(terms) > 1:
        terms = [a + b for a, b in zip(terms[::2], terms[1::2])]
    return terms[0]


def fold(ref, count):
    lane = lax.broadcasted_iota(jnp.int32, (count, LANES), 1)
    look = lane // 16
    source = look % 2 * 8 + look // 4 * 4 + lane // 8 % 2 * 2 + look // 2 % 2
    out = ref[pl.ds(0, count, stride=16), :]
    for pick in range(1, 16):
        out = jnp.where(source == pick, ref[pl.ds(pick, count, stride=16), :], out)
    return out * (1.0 / (LOOK_AZ * LOOK_RG))


def unpack_kernel(
    place_ref, own_ref, near_ref, far_ref, last_ref, window_ref,
    part_ref, root_ref,
    power_ref, date_ref,
):
    group = place_ref[0]
    dates_here = own_ref.shape[0]
    dates = part_ref.shape[0]
    row = lax.broadcasted_iota(jnp.int32, (8, LANES), 0)
    low = row < 4
    even = row % 2 == 0

    for offset, ref in enumerate((own_ref, near_ref, far_ref, last_ref)):
        base = (group ^ offset) * dates_here
        for index in range(dates_here):
            values = ref[index].astype(jnp.float32).reshape(8, 2, 8, LANES)
            for pick in range(2):
                squares = []
                for part in range(2):
                    lines = []
                    for look in (pick, pick + 2):
                        upper, lower = values[look, part], values[look + 4, part]
                        lines.append(
                            (
                                jnp.where(low, upper, pltpu.roll(lower, 4, 0)),
                                jnp.where(low, pltpu.roll(upper, 4, 0), lower),
                            )
                        )
                    for line in range(2):
                        first, second = lines[0][line], lines[1][line]
                        real = jnp.where(even, first, pltpu.roll(second, 1, 0))
                        imag = jnp.where(even, pltpu.roll(first, 7, 0), second)
                        part_ref[base + index, 0, pick, 2 * part + line] = real
                        part_ref[base + index, 1, pick, 2 * part + line] = imag
                        squares += [real * real, imag * imag]
                high, rest = rounded_parts(total(squares))
                power_ref[base + index, 8 * pick : 8 * pick + 8, :LANES] = high
                power_ref[base + index, 8 * pick : 8 * pick + 8, LANES:] = rest

    date_ref[...] = dot(power_ref[...].reshape(16 * dates, 2 * LANES), window_ref[...])
    root_ref[...] = lax.rsqrt(fold(date_ref, dates) + EPSILON)


def products_kernel(
    pair_ref, part_ref, root_ref, window_ref,
    out_ref,
    split_ref, sum_ref, scale_ref,
):
    owners = pair_ref.shape[0]
    pairs_here = pair_ref.shape[1] // 2
    pair_total = owners * pairs_here

    def split(target, slot, first, second):
        high, rest = rounded_parts(jnp.concatenate([first, second], axis=0))
        target[slot, :, :LANES] = high
        target[slot, :, LANES:] = rest

    def one_owner(owner, carry):
        for index in range(pairs_here):
            earlier = pair_ref[owner, index]
            later = pair_ref[owner, pairs_here + index]
            real, imag = [], []
            for pick in range(2):
                dot_terms, cross_terms = [], []
                for line in range(LOOK_AZ):
                    left_real = part_ref[earlier, 0, pick, line]
                    left_imag = part_ref[earlier, 1, pick, line]
                    right_real = part_ref[later, 0, pick, line]
                    right_imag = part_ref[later, 1, pick, line]
                    dot_terms += [left_real * right_real, left_imag * right_imag]
                    cross_terms += [left_imag * right_real - left_real * right_imag]
                real.append(total(dot_terms))
                imag.append(total(cross_terms))
            slot = 2 * (owner * pairs_here + index)
            split(split_ref, slot, *real)
            split(split_ref, slot + 1, *imag)
        return carry

    lax.fori_loop(0, owners, one_owner, 0, unroll=owners)
    sum_ref[...] = dot(split_ref[...].reshape(32 * pair_total, 2 * LANES), window_ref[...])
    for owner in range(owners):
        for index in range(pairs_here):
            earlier = root_ref[pl.ds(pair_ref[owner, index], 1), :]
            later = root_ref[pl.ds(pair_ref[owner, pairs_here + index], 1), :]
            start = 2 * (owner * pairs_here + index)
            scale_ref[start : start + 2, :] = jnp.broadcast_to(earlier * later, (2, LANES))
    ratio = fold(sum_ref, 2 * pair_total) * scale_ref[...]
    out_ref[...] = ratio.reshape(out_ref.shape)


def filter_kernel(
    ratio_ref, sample_ref, place_table_ref, line_ref, back_ref, end_ref,
    filtered_ref, coherence_ref, high_ref, low_ref, size_ref,
):
    pairs = coherence_ref.shape[0]
    lane = lax.broadcasted_iota(jnp.int32, (8, LANES), 1)
    line = lax.broadcasted_iota(jnp.int32, (8, LANES), 0)
    inside = lane // 16 == line
    sources = ratio_ref.shape[0]
    values = ratio_ref[...].reshape(sources * 2 * pairs, LANES)
    square = values * values
    size = jnp.sqrt(square + pltpu.roll(square, square.shape[0] - 1, 0))

    def place(target, start, column, row):
        target[start : start + 8, column * LANES : (column + 1) * LANES] = jnp.where(
            inside, jnp.broadcast_to(row, (8, LANES)), 0.0
        ).astype(target.dtype)

    high = values.astype(jnp.bfloat16).astype(jnp.float32)
    low = values - high
    for source in range(sources):
        core = source & 1
        half = (source >> 1) & 1
        block = core * 4 + (source >> 2)
        for pair in range(pairs):
            start = pair * PATCH + block * 8
            first = (source * pairs + pair) * 2
            for part in range(2):
                pick = slice(first + part, first + part + 1)
                place(high_ref, start, 2 * part + half, high[pick])
                place(low_ref, start, 2 * part + half, low[pick])
            place(size_ref, start, half, size[first : first + 1])
    for pair in range(pairs):
        lines = slice(pair * PATCH, (pair + 1) * PATCH)
        magnitude = dot_rows(place_table_ref[...], size_ref[lines])
        coherence_ref[pair] = magnitude.astype(coherence_ref.dtype)
    spread = dot(
        jnp.concatenate([high_ref[...], low_ref[...], high_ref[...]], 1), sample_ref[...]
    )
    left = lax.broadcasted_iota(jnp.int32, (HALF, LANES), 1) < PATCH
    columns = []
    for half in range(2):
        first = spread[half * HALF : (half + 1) * HALF]
        second = spread[PATCH + half * HALF : PATCH + (half + 1) * HALF]
        real = jnp.where(left, first, pltpu.roll(second, PATCH, 1))
        imag = jnp.where(left, pltpu.roll(first, PATCH, 1), second)
        columns.append(jnp.concatenate([real, imag], 0))
        columns.append(jnp.concatenate([imag, -real], 0))
    spectrum = dot(line_ref[...], three_parts(jnp.concatenate(columns, 1), 0))
    top_real, top_imag, low_real, low_imag = (
        spectrum[:, index * LANES : (index + 1) * LANES] for index in range(4)
    )
    sign = 1.0 - 2.0 * (lax.broadcasted_iota(jnp.int32, (PATCH, LANES), 0) % 2).astype(jnp.float32)
    side = lax.broadcasted_iota(jnp.int32, (1, LANES), 1) < PATCH
    weighted = []
    for real, imag in (
        (top_real, top_imag),
        (top_real + sign * low_real, top_imag + sign * low_imag),
        (low_real, low_imag),
    ):
        weight = lax.rsqrt(lax.rsqrt(real * real + imag * imag + 1.0))
        total = jnp.sum(weight, axis=0, keepdims=True)
        first = jnp.sum(jnp.where(side, total, 0.0), axis=1, keepdims=True)
        second = jnp.sum(jnp.where(side, 0.0, total), axis=1, keepdims=True)
        weight = weight * ((1.0 * PATCH * PATCH) / jnp.where(side, first, second))
        weighted.append(three_parts(jnp.concatenate([real * weight, imag * weight], 1), 1))
    back = dot_rows(
        back_ref[...],
        jnp.concatenate([weighted[0], weighted[1], weighted[1], weighted[2]], 0),
    )
    count = back.shape[0] // 2
    lines = dot(
        three_parts(jnp.concatenate([back[:count], back[count:]], 1), 1), end_ref[...]
    )
    filtered_ref[...] = lines[:, :PATCH].reshape(filtered_ref.shape).astype(filtered_ref.dtype)


def fast_local(acquisitions, date_pairs, sizes):
    depth, across, cores = sizes
    total = depth * across * cores
    dates_here, line_count, _, sample_count = acquisitions.shape
    columns = sample_count // LANES
    lines_each = line_count // depth
    rows = lines_each * columns * 2
    look_lines = lines_each // LOOK_AZ
    look_samples = sample_count // LOOK_RG
    cells = look_lines * look_samples
    pairs_here = date_pairs.shape[1]
    pair_total = pairs_here * total
    dates = dates_here * depth
    group = lax.axis_index("date")
    names = ("date", "rng", "az")

    def swap(values, offset):
        return lax.ppermute(values, names, [(i, i ^ offset) for i in range(total)])

    view = acquisitions.reshape(dates_here, line_count, 2, columns, LANES)
    view = view.transpose(0, 1, 3, 2, 4).reshape(dates_here, line_count * columns * 2, LANES)

    step = across * cores
    vmem = pl.BlockSpec(memory_space=pltpu.VMEM)
    smem = pl.BlockSpec(memory_space=pltpu.SMEM)

    def block(offset):
        return lax.dynamic_slice_in_dim(view, (group ^ offset) * rows, rows, 1)

    received = {offset: swap(block(offset), offset * step) for offset in (3, 1, 2)}
    own = block(0)
    listed = jnp.broadcast_to(date_pairs.reshape(1, -1), (total, 2 * pairs_here))
    pair_list = lax.all_to_all(listed, names, 0, 0, tiled=True)
    window = jnp.asarray(window_table(cells))
    parts, roots = pl.pallas_call(
        unpack_kernel,
        name="unpack",
        out_shape=[
            jax.ShapeDtypeStruct((dates, 2, 2, LOOK_AZ, 8, LANES), jnp.float32),
            jax.ShapeDtypeStruct((dates, cells), jnp.float32),
        ],
        in_specs=[smem] + [vmem] * 5,
        out_specs=[vmem] * 2,
        scratch_shapes=[
            pltpu.VMEM((dates, 16, 2 * LANES), jnp.bfloat16),
            pltpu.VMEM((16 * dates, cells), jnp.float32),
        ],
        compiler_params=pltpu.CompilerParams(vmem_limit_bytes=8 << 20),
    )(group.reshape(1), own, received[1], received[2], received[3], window)
    ratios = pl.pallas_call(
        products_kernel,
        name="products",
        out_shape=jax.ShapeDtypeStruct((total, 2 * pairs_here, cells), jnp.float32),
        in_specs=[smem] + [vmem] * 3,
        out_specs=vmem,
        scratch_shapes=[
            pltpu.VMEM((2 * pair_total, 16, 2 * LANES), jnp.bfloat16),
            pltpu.VMEM((32 * pair_total, cells), jnp.float32),
            pltpu.VMEM((2 * pair_total, cells), jnp.float32),
        ],
        compiler_params=pltpu.CompilerParams(vmem_limit_bytes=8 << 20),
    )(pair_list, parts, roots, window)
    arrived = lax.all_to_all(ratios, names, 0, 0, tiled=True)
    sample_table, place_table = sample_tables(cells, look_samples, across)
    line_table, end_table = line_tables()
    tables = [
        split_table(sample_table, 0),
        place_table,
        split_table(line_table, 1),
        split_table(back_table(pairs_here), 1),
        split_table(end_table, 0),
    ]
    filtered, coherence = pl.pallas_call(
        filter_kernel,
        name="filter",
        out_shape=[
            jax.ShapeDtypeStruct((pairs_here, 2, HALF, PATCH), jnp.bfloat16),
            jax.ShapeDtypeStruct((pairs_here, HALF, PATCH), jnp.bfloat16),
        ],
        in_specs=[vmem] * (1 + len(tables)),
        out_specs=[vmem, vmem],
        scratch_shapes=[
            pltpu.VMEM((pairs_here * PATCH, 2 * across * cells), jnp.bfloat16),
            pltpu.VMEM((pairs_here * PATCH, 2 * across * cells), jnp.bfloat16),
            pltpu.VMEM((pairs_here * PATCH, across * cells), jnp.bfloat16),
        ],
        compiler_params=pltpu.CompilerParams(vmem_limit_bytes=8 << 20),
    )(arrived, *[jnp.asarray(t) for t in tables])
    return (filtered.transpose(0, 1, 3, 2), coherence.transpose(0, 2, 1))


def fits(acquisitions, date_pairs, sizes):
    depth, across, cores = sizes
    _, line_count, _, sample_count = acquisitions.shape
    look_lines = line_count // depth // LOOK_AZ
    look_samples = sample_count // LOOK_RG
    return (
        sizes == (4, 2, 2)
        and line_count % (depth * LOOK_AZ) == 0
        and sample_count == 2 * LANES
        and look_lines == 8
        and look_lines * look_samples == LANES
        and line_count * cores == LOOK_AZ * PATCH
        and sample_count * across == LOOK_RG * HALF
        and date_pairs.shape[1] == 2
    )


def solution(mesh):
    sizes = tuple(mesh.shape[name] for name in ("date", "rng", "az"))

    def chosen(acquisitions, date_pairs):
        if fits(acquisitions, date_pairs, sizes):
            return fast_local(acquisitions, date_pairs, sizes)
        return local(acquisitions, date_pairs)

    return jax.shard_map(
        chosen,
        mesh=mesh,
        in_specs=(P(("tile", "date"), "az", None, "rng"), P(None, ("date", "rng", "az"))),
        out_specs=(
            P(("tile", "date", "rng", "az"), None, None, None),
            P(("tile", "date", "rng", "az"), None, None),
        ),
        check_vma=False,
    )
```

```python
import math

import jax
import jax.numpy as jnp
import numpy as np
from jax import lax
from jax.experimental import pallas as pl
from jax.experimental.pallas import tpu as pltpu
from jax.sharding import PartitionSpec as P


PATCH = 64
LOOK_AZ = 4
LOOK_RG = 16
HALF = 32
LANES = 128
SHIFTS = (1, 2, 3)


EPSILON = 1e-06
HIGHEST = lax.Precision.HIGHEST


def fourier_tables(length):
    position = jnp.arange(length, dtype=jnp.int32)
    product = position[:, None] * position[None, :] % length
    angle = product.astype(jnp.float32) * (2.0 * math.pi / length)
    return (jnp.cos(angle), jnp.sin(angle))


def taper_window(length):
    midway = length // 2
    position = jnp.arange(length, dtype=jnp.float32)
    ramp_line = 1.0 - jnp.abs(position + 0.5 - midway) / midway
    return ramp_line[:, None] * ramp_line[None, :]


def transform(real_part, imag_part, cosine_table, sine_table, inverse):
    length = cosine_table.shape[0]
    if inverse:
        matrix = jnp.concatenate(
            [
                jnp.concatenate([cosine_table, sine_table], 1),
                jnp.concatenate([-sine_table, cosine_table], 1),
            ],
            0,
        )
    else:
        matrix = jnp.concatenate(
            [
                jnp.concatenate([cosine_table, -sine_table], 1),
                jnp.concatenate([sine_table, cosine_table], 1),
            ],
            0,
        )
    joined = jnp.concatenate([real_part, imag_part], axis=-1)
    across = jnp.einsum("bnc,cd->bnd", joined, matrix, precision=HIGHEST)
    rotated = jnp.einsum(
        "tkn,bnd->btkd", jnp.stack([cosine_table, sine_table]), across, precision=HIGHEST
    )
    with_cosine = rotated[:, 0]
    with_sine = rotated[:, 1]
    if inverse:
        scaling = 1.0 / (length * length)
        out_real = (with_cosine[..., :length] - with_sine[..., length:]) * scaling
        out_imag = (with_cosine[..., length:] + with_sine[..., :length]) * scaling
    else:
        out_real = with_cosine[..., :length] + with_sine[..., length:]
        out_imag = with_cosine[..., length:] - with_sine[..., :length]
    return (out_real, out_imag)


def goldstein(
    extended_real, extended_imag, cosine_table, sine_table, window, block_lines, block_samples
):
    groups = extended_real.shape[0]
    extent_line = extended_real.shape[1]
    extent_sample = extended_real.shape[2]
    length = cosine_table.shape[0]
    midway = length // 2
    summed_real = jnp.zeros_like(extended_real)
    summed_imag = jnp.zeros_like(extended_imag)
    for start_line in (0, midway):
        for start_sample in (0, midway):
            count_line = (extent_line - start_line) // length
            count_sample = (extent_sample - start_sample) // length
            stop_line = start_line + count_line * length
            stop_sample = start_sample + count_sample * length

            def extract(values):
                region = values[:, start_line:stop_line, start_sample:stop_sample]
                region = region.reshape(groups, count_line, length, count_sample, length)
                return region.transpose(0, 1, 3, 2, 4).reshape(-1, length, length)

            def insert(values):
                shaped = (values * window).reshape(groups, count_line, count_sample, length, length)
                return shaped.transpose(0, 1, 3, 2, 4).reshape(
                    groups, count_line * length, count_sample * length
                )

            spec_real, spec_imag = transform(
                extract(extended_real), extract(extended_imag), cosine_table, sine_table, False
            )
            energy = spec_real * spec_real + spec_imag * spec_imag
            weight = (energy + 1.0) ** 0.25
            weight = weight / jnp.mean(weight, axis=(1, 2), keepdims=True)
            back_real, back_imag = transform(
                spec_real * weight, spec_imag * weight, cosine_table, sine_table, True
            )
            summed_real = summed_real.at[:, start_line:stop_line, start_sample:stop_sample].add(
                insert(back_real)
            )
            summed_imag = summed_imag.at[:, start_line:stop_line, start_sample:stop_sample].add(
                insert(back_imag)
            )
    center_real = summed_real[:, midway : midway + block_lines, midway : midway + block_samples]
    center_imag = summed_imag[:, midway : midway + block_lines, midway : midway + block_samples]
    return (center_real, center_imag)


def local(acquisitions, date_pairs):
    every_pair = lax.all_gather(date_pairs, ("date", "rng", "az"), axis=1, tiled=True)
    by_lines = lax.all_to_all(acquisitions, "date", split_axis=1, concat_axis=0, tiled=True)
    line_count = by_lines.shape[1]
    sample_count = by_lines.shape[3]
    look_lines = line_count // LOOK_AZ
    look_samples = sample_count // LOOK_RG

    def take_looks(values):
        leading = values.shape[:-2]
        shaped = values.reshape(leading + (look_lines, LOOK_AZ, look_samples, LOOK_RG))
        return jnp.sum(shaped, axis=(-3, -1)) * (1.0 / (LOOK_AZ * LOOK_RG))

    real_lines = by_lines[:, :, 0, :].astype(jnp.float32)
    imag_lines = by_lines[:, :, 1, :].astype(jnp.float32)
    intensity = take_looks(real_lines * real_lines + imag_lines * imag_lines)
    pair_total = every_pair.shape[1]
    block_rows = math.gcd(pair_total, 32)
    turns = pair_total // block_rows
    earlier = every_pair[0].reshape(turns, block_rows)
    later = every_pair[1].reshape(turns, block_rows)

    def cross_block(indices):
        left = jnp.take(by_lines, indices[0], axis=0).astype(jnp.float32)
        right = jnp.take(by_lines, indices[1], axis=0).astype(jnp.float32)
        cross_real = take_looks(left[:, :, 0] * right[:, :, 0] + left[:, :, 1] * right[:, :, 1])
        cross_imag = take_looks(left[:, :, 1] * right[:, :, 0] - left[:, :, 0] * right[:, :, 1])
        return (cross_real, cross_imag)

    cross_real, cross_imag = lax.map(cross_block, (earlier, later))
    cross_real = cross_real.reshape(pair_total, look_lines, look_samples)
    cross_imag = cross_imag.reshape(pair_total, look_lines, look_samples)
    power_early = jnp.take(intensity, every_pair[0], axis=0)
    power_late = jnp.take(intensity, every_pair[1], axis=0)
    denominator = jnp.sqrt((power_early + EPSILON) * (power_late + EPSILON))
    payload = jnp.stack([cross_real / denominator, cross_imag / denominator], axis=1)
    partway = lax.all_to_all(
        lax.all_to_all(payload, "date", split_axis=0, concat_axis=2, tiled=True),
        "rng",
        split_axis=0,
        concat_axis=3,
        tiled=True,
    )
    returned = lax.all_to_all(partway, "az", split_axis=0, concat_axis=2, tiled=True)
    ratio_real = returned[:, 0]
    ratio_imag = returned[:, 1]
    coherence = jnp.sqrt(ratio_real * ratio_real + ratio_imag * ratio_imag).astype(jnp.bfloat16)
    block_lines = ratio_real.shape[1]
    block_samples = ratio_real.shape[2]
    padding = ((0, 0), (HALF, HALF), (HALF, HALF))
    extended_real = jnp.pad(ratio_real, padding)
    extended_imag = jnp.pad(ratio_imag, padding)
    cosine_table, sine_table = fourier_tables(PATCH)
    window = taper_window(PATCH)
    out_real, out_imag = goldstein(
        extended_real, extended_imag, cosine_table, sine_table, window, block_lines, block_samples
    )
    filtered = jnp.stack([out_real, out_imag], axis=1).astype(jnp.bfloat16)
    return (filtered, coherence)


def rounded_parts(values):
    high = values.astype(jnp.bfloat16)
    low = (values - high.astype(jnp.float32)).astype(jnp.bfloat16)
    return (high, low)


def split_table(table, axis):
    table = np.asarray(table, np.float32)
    high = table.astype(jnp.bfloat16)
    low = (table - high.astype(np.float32)).astype(jnp.bfloat16)
    return np.concatenate([high, high, low], axis)


def three_parts(values, axis):
    high, low = rounded_parts(values)
    return jnp.concatenate([high, low, high], axis)


def window_table(cells):
    lane = np.arange(LANES)
    table = lane[:, None] // LOOK_RG == np.arange(cells)[None, :] % (LANES // LOOK_RG)
    return np.concatenate([table, table], 0).astype(np.float32).astype(jnp.bfloat16)


def sample_tables(cells, samples, halves):
    cell = np.arange(cells) % samples
    frequency = np.arange(PATCH)
    forward = []
    place = []
    for half in range(halves):
        position = half * samples + cell
        angle = 2.0 * np.pi * (position[:, None] * frequency[None, :] % PATCH) / PATCH
        forward.append((np.cos(angle), np.sin(angle)))
        place.append(np.arange(halves * samples)[:, None] == position[None, :])
    real = [np.concatenate([c, -s], 1) for c, s in forward]
    imag = [np.concatenate([s, c], 1) for c, s in forward]
    return (
        np.concatenate(real + imag, 0),
        np.concatenate(place, 1).astype(np.float32).astype(jnp.bfloat16),
    )


def line_tables():
    row = np.arange(HALF)
    frequency = np.arange(PATCH)
    angle = 2.0 * np.pi * (frequency[:, None] * row[None, :] % PATCH) / PATCH
    cosine, sine = np.cos(angle), np.sin(angle)
    ramp = 1.0 - np.abs(np.arange(PATCH) + 0.5 - HALF) / HALF
    first, second = ramp[None, :HALF], ramp[None, HALF:]
    flip = (1.0 - 2.0 * (frequency % 2))[:, None]
    none = np.zeros_like(angle)

    def back(wave):
        top = np.concatenate([second * wave, first * wave, none, none], 0)
        bottom = np.concatenate([none, none, second * flip * wave, first * wave], 0)
        return np.concatenate([top, bottom], 1)

    end = np.concatenate([back(cosine), back(sine)], 0) / PATCH**2
    end = np.concatenate([end, np.zeros((end.shape[0], 2 * LANES - PATCH))], 1)
    return (np.concatenate([cosine, sine], 1), end)


def back_table(pairs):
    frequency = np.arange(PATCH)
    column = np.arange(HALF)
    angle = 2.0 * np.pi * (column[:, None] * frequency[None, :] % PATCH) / PATCH
    c, s = np.cos(angle), np.sin(angle)
    direct = np.concatenate([np.concatenate([c, -s], 1), np.concatenate([s, c], 1)], 0)
    turned = np.concatenate([np.concatenate([-s, -c], 1), np.concatenate([c, -s], 1)], 0)
    identity = np.eye(pairs)
    table = np.concatenate([np.kron(identity, direct), np.kron(identity, turned)], 0)
    table = table.reshape(-1, pairs, 2, PATCH).transpose(0, 2, 1, 3)
    return table.reshape(-1, 2 * pairs * PATCH)


def dot(left, right):
    return jnp.dot(left, right, preferred_element_type=jnp.float32)


def dot_rows(left, right):
    return lax.dot_general(
        left, right, (((1,), (1,)), ((), ())), preferred_element_type=jnp.float32
    )


def total(terms):
    while len(terms) > 1:
        terms = [a + b for a, b in zip(terms[::2], terms[1::2])]
    return terms[0]


def fold(ref, count):
    lane = lax.broadcasted_iota(jnp.int32, (count, LANES), 1)
    look = lane // 16
    source = look % 2 * 8 + look // 4 * 4 + lane // 8 % 2 * 2 + look // 2 % 2
    out = ref[pl.ds(0, count, stride=16), :]
    for pick in range(1, 16):
        out = jnp.where(source == pick, ref[pl.ds(pick, count, stride=16), :], out)
    return out * (1.0 / (LOOK_AZ * LOOK_RG))


def unpack_kernel(
    place_ref, own_ref, first_ref, second_ref, third_ref, window_ref,
    part_ref, root_ref,
    power_ref, date_ref,
):
    group = place_ref[0]
    dates_here = own_ref.shape[0]
    dates = part_ref.shape[0]
    depth = dates // dates_here
    row = lax.broadcasted_iota(jnp.int32, (8, LANES), 0)
    low = row < 4
    even = row % 2 == 0

    for shift, ref in zip((0, *SHIFTS), (own_ref, first_ref, second_ref, third_ref)):
        base = lax.rem(group + depth - shift, depth) * dates_here
        for index in range(dates_here):
            values = ref[index].astype(jnp.float32).reshape(8, 2, 8, LANES)
            for pick in range(2):
                squares = []
                for part in range(2):
                    lines = []
                    for look in (pick, pick + 2):
                        upper, lower = values[look, part], values[look + 4, part]
                        lines.append(
                            (
                                jnp.where(low, upper, pltpu.roll(lower, 4, 0)),
                                jnp.where(low, pltpu.roll(upper, 4, 0), lower),
                            )
                        )
                    for line in range(2):
                        first, second = lines[0][line], lines[1][line]
                        real = jnp.where(even, first, pltpu.roll(second, 1, 0))
                        imag = jnp.where(even, pltpu.roll(first, 7, 0), second)
                        part_ref[base + index, 0, pick, 2 * part + line] = real
                        part_ref[base + index, 1, pick, 2 * part + line] = imag
                        squares += [real * real, imag * imag]
                high, rest = rounded_parts(total(squares))
                power_ref[base + index, 8 * pick : 8 * pick + 8, :LANES] = high
                power_ref[base + index, 8 * pick : 8 * pick + 8, LANES:] = rest

    date_ref[...] = dot(power_ref[...].reshape(16 * dates, 2 * LANES), window_ref[...])
    root_ref[...] = lax.rsqrt(fold(date_ref, dates) + EPSILON)


def products_kernel(
    pair_ref, part_ref, root_ref, window_ref,
    out_ref,
    split_ref, sum_ref, scale_ref,
):
    owners = pair_ref.shape[0]
    pairs_here = pair_ref.shape[1] // 2
    pair_total = owners * pairs_here

    def split(target, slot, first, second):
        high, rest = rounded_parts(jnp.concatenate([first, second], axis=0))
        target[slot, :, :LANES] = high
        target[slot, :, LANES:] = rest

    def one_owner(owner, carry):
        for index in range(pairs_here):
            earlier = pair_ref[owner, index]
            later = pair_ref[owner, pairs_here + index]
            real, imag = [], []
            for pick in range(2):
                dot_terms, cross_terms = [], []
                for line in range(LOOK_AZ):
                    left_real = part_ref[earlier, 0, pick, line]
                    left_imag = part_ref[earlier, 1, pick, line]
                    right_real = part_ref[later, 0, pick, line]
                    right_imag = part_ref[later, 1, pick, line]
                    dot_terms += [left_real * right_real, left_imag * right_imag]
                    cross_terms += [left_imag * right_real - left_real * right_imag]
                real.append(total(dot_terms))
                imag.append(total(cross_terms))
            slot = 2 * (owner * pairs_here + index)
            split(split_ref, slot, *real)
            split(split_ref, slot + 1, *imag)
        return carry

    lax.fori_loop(0, owners, one_owner, 0, unroll=owners)
    sum_ref[...] = dot(split_ref[...].reshape(32 * pair_total, 2 * LANES), window_ref[...])
    for owner in range(owners):
        for index in range(pairs_here):
            earlier = root_ref[pl.ds(pair_ref[owner, index], 1), :]
            later = root_ref[pl.ds(pair_ref[owner, pairs_here + index], 1), :]
            start = 2 * (owner * pairs_here + index)
            scale_ref[start : start + 2, :] = jnp.broadcast_to(earlier * later, (2, LANES))
    ratio = fold(sum_ref, 2 * pair_total) * scale_ref[...]
    out_ref[...] = ratio.reshape(out_ref.shape)


def filter_kernel(
    ratio_ref, sample_ref, place_table_ref, line_ref, back_ref, end_ref,
    filtered_ref, coherence_ref, high_ref, low_ref, size_ref,
):
    pairs = coherence_ref.shape[0]
    lane = lax.broadcasted_iota(jnp.int32, (8, LANES), 1)
    line = lax.broadcasted_iota(jnp.int32, (8, LANES), 0)
    inside = lane // 16 == line
    sources = ratio_ref.shape[0]
    values = ratio_ref[...].reshape(sources * 2 * pairs, LANES)
    square = values * values
    size = jnp.sqrt(square + pltpu.roll(square, square.shape[0] - 1, 0))

    def place(target, start, column, row):
        target[start : start + 8, column * LANES : (column + 1) * LANES] = jnp.where(
            inside, jnp.broadcast_to(row, (8, LANES)), 0.0
        ).astype(target.dtype)

    high = values.astype(jnp.bfloat16).astype(jnp.float32)
    low = values - high
    for source in range(sources):
        core = source & 1
        half = (source >> 1) & 1
        block = core * 4 + (source >> 2)
        for pair in range(pairs):
            start = pair * PATCH + block * 8
            first = (source * pairs + pair) * 2
            for part in range(2):
                pick = slice(first + part, first + part + 1)
                place(high_ref, start, 2 * part + half, high[pick])
                place(low_ref, start, 2 * part + half, low[pick])
            place(size_ref, start, half, size[first : first + 1])
    for pair in range(pairs):
        lines = slice(pair * PATCH, (pair + 1) * PATCH)
        magnitude = dot_rows(place_table_ref[...], size_ref[lines])
        coherence_ref[pair] = magnitude.astype(coherence_ref.dtype)
    spread = dot(
        jnp.concatenate([high_ref[...], low_ref[...], high_ref[...]], 1), sample_ref[...]
    )
    left = lax.broadcasted_iota(jnp.int32, (HALF, LANES), 1) < PATCH
    columns = []
    for half in range(2):
        first = spread[half * HALF : (half + 1) * HALF]
        second = spread[PATCH + half * HALF : PATCH + (half + 1) * HALF]
        real = jnp.where(left, first, pltpu.roll(second, PATCH, 1))
        imag = jnp.where(left, pltpu.roll(first, PATCH, 1), second)
        columns.append(jnp.concatenate([real, imag], 0))
        columns.append(jnp.concatenate([imag, -real], 0))
    spectrum = dot(line_ref[...], three_parts(jnp.concatenate(columns, 1), 0))
    top_real, top_imag, low_real, low_imag = (
        spectrum[:, index * LANES : (index + 1) * LANES] for index in range(4)
    )
    sign = 1.0 - 2.0 * (lax.broadcasted_iota(jnp.int32, (PATCH, LANES), 0) % 2).astype(jnp.float32)
    side = lax.broadcasted_iota(jnp.int32, (1, LANES), 1) < PATCH
    weighted = []
    for real, imag in (
        (top_real, top_imag),
        (top_real + sign * low_real, top_imag + sign * low_imag),
        (low_real, low_imag),
    ):
        weight = lax.rsqrt(lax.rsqrt(real * real + imag * imag + 1.0))
        total = jnp.sum(weight, axis=0, keepdims=True)
        first = jnp.sum(jnp.where(side, total, 0.0), axis=1, keepdims=True)
        second = jnp.sum(jnp.where(side, 0.0, total), axis=1, keepdims=True)
        weight = weight * ((1.0 * PATCH * PATCH) / jnp.where(side, first, second))
        weighted.append(three_parts(jnp.concatenate([real * weight, imag * weight], 1), 1))
    back = dot_rows(
        back_ref[...],
        jnp.concatenate([weighted[0], weighted[1], weighted[1], weighted[2]], 0),
    )
    count = back.shape[0] // 2
    lines = dot(
        three_parts(jnp.concatenate([back[:count], back[count:]], 1), 1), end_ref[...]
    )
    filtered_ref[...] = lines[:, :PATCH].reshape(filtered_ref.shape).astype(filtered_ref.dtype)


def fast_local(acquisitions, date_pairs, sizes):
    depth, across, cores = sizes
    total = depth * across * cores
    dates_here, line_count, _, sample_count = acquisitions.shape
    columns = sample_count // LANES
    lines_each = line_count // depth
    rows = lines_each * columns * 2
    look_lines = lines_each // LOOK_AZ
    look_samples = sample_count // LOOK_RG
    cells = look_lines * look_samples
    pairs_here = date_pairs.shape[1]
    pair_total = pairs_here * total
    dates = dates_here * depth
    group = lax.axis_index("date")
    names = ("date", "rng", "az")

    view = acquisitions.reshape(dates_here, line_count, 2, columns, LANES)
    view = view.transpose(0, 1, 3, 2, 4).reshape(dates_here, line_count * columns * 2, LANES)

    step = across * cores
    vmem = pl.BlockSpec(memory_space=pltpu.VMEM)
    smem = pl.BlockSpec(memory_space=pltpu.SMEM)

    def block(shift):
        return lax.dynamic_slice_in_dim(view, lax.rem(group + shift, depth) * rows, rows, 1)

    received = []
    for shift in SHIFTS:
        received.append(
            lax.ppermute(
                block(shift), names, [(i, (i + shift * step) % total) for i in range(total)]
            )
        )
    own = block(0)
    listed = jnp.broadcast_to(date_pairs.reshape(1, -1), (total, 2 * pairs_here))
    pair_list = lax.all_to_all(listed, names, 0, 0, tiled=True)
    window = jnp.asarray(window_table(cells))
    parts, roots = pl.pallas_call(
        unpack_kernel,
        name="unpack",
        out_shape=[
            jax.ShapeDtypeStruct((dates, 2, 2, LOOK_AZ, 8, LANES), jnp.float32),
            jax.ShapeDtypeStruct((dates, cells), jnp.float32),
        ],
        in_specs=[smem] + [vmem] * 5,
        out_specs=[vmem] * 2,
        scratch_shapes=[
            pltpu.VMEM((dates, 16, 2 * LANES), jnp.bfloat16),
            pltpu.VMEM((16 * dates, cells), jnp.float32),
        ],
        compiler_params=pltpu.CompilerParams(vmem_limit_bytes=8 << 20),
    )(group.reshape(1), own, *received, window)
    ratios = pl.pallas_call(
        products_kernel,
        name="products",
        out_shape=jax.ShapeDtypeStruct((total, 2 * pairs_here, cells), jnp.float32),
        in_specs=[smem] + [vmem] * 3,
        out_specs=vmem,
        scratch_shapes=[
            pltpu.VMEM((2 * pair_total, 16, 2 * LANES), jnp.bfloat16),
            pltpu.VMEM((32 * pair_total, cells), jnp.float32),
            pltpu.VMEM((2 * pair_total, cells), jnp.float32),
        ],
        compiler_params=pltpu.CompilerParams(vmem_limit_bytes=8 << 20),
    )(pair_list, parts, roots, window)
    arrived = lax.all_to_all(ratios, names, 0, 0, tiled=True)
    sample_table, place_table = sample_tables(cells, look_samples, across)
    line_table, end_table = line_tables()
    tables = [
        split_table(sample_table, 0),
        place_table,
        split_table(line_table, 1),
        split_table(back_table(pairs_here), 1),
        split_table(end_table, 0),
    ]
    filtered, coherence = pl.pallas_call(
        filter_kernel,
        name="filter",
        out_shape=[
            jax.ShapeDtypeStruct((pairs_here, 2, HALF, PATCH), jnp.bfloat16),
            jax.ShapeDtypeStruct((pairs_here, HALF, PATCH), jnp.bfloat16),
        ],
        in_specs=[vmem] * (1 + len(tables)),
        out_specs=[vmem, vmem],
        scratch_shapes=[
            pltpu.VMEM((pairs_here * PATCH, 2 * across * cells), jnp.bfloat16),
            pltpu.VMEM((pairs_here * PATCH, 2 * across * cells), jnp.bfloat16),
            pltpu.VMEM((pairs_here * PATCH, across * cells), jnp.bfloat16),
        ],
        compiler_params=pltpu.CompilerParams(vmem_limit_bytes=8 << 20),
    )(arrived, *[jnp.asarray(t) for t in tables])
    return (filtered.transpose(0, 1, 3, 2), coherence.transpose(0, 2, 1))


def fits(acquisitions, date_pairs, sizes):
    depth, across, cores = sizes
    _, line_count, _, sample_count = acquisitions.shape
    look_lines = line_count // depth // LOOK_AZ
    look_samples = sample_count // LOOK_RG
    return (
        sizes == (4, 2, 2)
        and line_count % (depth * LOOK_AZ) == 0
        and sample_count == 2 * LANES
        and look_lines == 8
        and look_lines * look_samples == LANES
        and line_count * cores == LOOK_AZ * PATCH
        and sample_count * across == LOOK_RG * HALF
        and date_pairs.shape[1] == 2
    )


def solution(mesh):
    sizes = tuple(mesh.shape[name] for name in ("date", "rng", "az"))

    def chosen(acquisitions, date_pairs):
        if fits(acquisitions, date_pairs, sizes):
            return fast_local(acquisitions, date_pairs, sizes)
        return local(acquisitions, date_pairs)

    return jax.shard_map(
        chosen,
        mesh=mesh,
        in_specs=(P(("tile", "date"), "az", None, "rng"), P(None, ("date", "rng", "az"))),
        out_specs=(
            P(("tile", "date", "rng", "az"), None, None, None),
            P(("tile", "date", "rng", "az"), None, None),
        ),
        check_vma=False,
    )
```
